32 devices in a mesh: groups: 2 (over y), row: 4 (over z), col: 4 (over x, core).
Axes of the slice: x: 2, y: 2, z: 4, core: 2. Of those that a mesh axis runs over, the one named last changes fastest.
Arguments:
- queries: bfloat16 [8, 512, 512], P(('groups', 'col'), 'row'), parts along dimension 0, may hold values from -6 to 6
- keys: bfloat16 [8, 512, 128], P(('groups', 'row'), 'col'), parts along dimension 0, may hold values from -6 to 6
- values: bfloat16 [8, 512, 128], P(('groups', 'row'), 'col'), parts along dimension 0, may hold values from -6 to 6
- block_list: int32 [8, 4, 4, 4], P('groups'), parts along dimension 0, may hold values from 0 to 3, as said below
- block_count: int32 [8, 4, 4], P('groups'), parts along dimension 0, may hold values from 0 to 4, as said below
Outputs:
- attended: bfloat16 [8, 512, 512], P(('groups', 'col'), 'row'), parts along dimension 0
The draws below stay inside these ranges and needn't reach their ends.
There are 2 independent parts, one for each index of `groups`. The reference program is written for one: setup_inputs(seed, part) draws one part's arguments, and reference() takes and returns one part's arrays. A program takes and returns all parts, laid end to end along the dimension named above; each array names one. Nothing has to cross between parts.
Inputs may be any that keep to these rules, and one draw needn't show every extreme that they name: For query block i = c * 4 + q, the first block_count[c, q, r] entries of block_list[c, q, r] are distinct positions j in increasing order of key blocks r * 4 + j that do not lie after block i; block i itself is always listed in its panel; the remaining entries are other positions of the panel and carry no meaning. `block_count`: some query block lists all 4 blocks of some panel in every draw.
All inputs are finite; a program needn't handle non-finite values.
Results may differ from the reference program's by a relative error of at most 0.0036.
Values may be sent and summed in bfloat16 or wider, within the bound.
A program may use at most 64 MiB of HBM per device.

```python
import jax
import jax.numpy as jnp
from jax import lax

BLOCK = 128
HD = 128
GROUP = 4
QP = 512
KP = 512
QBP = 4
KBP = 4
SEQ = 2048
N_ROW = 4
N_COL = 4


def active_blocks(key):
    total_blocks = SEQ // BLOCK
    vert_key, slash_key = jax.random.split(jax.random.fold_in(key, 11))
    vertical = jax.random.randint(vert_key, (total_blocks,), 0, 8) == 0
    vertical = vertical.at[0].set(True)
    slash_hit = jax.random.randint(slash_key, (total_blocks,), 0, 16) == 0
    query_index = jnp.arange(total_blocks, dtype=jnp.int32)[:, None]
    key_index = jnp.arange(total_blocks, dtype=jnp.int32)[None, :]
    distance = query_index - key_index
    near = distance < KBP
    diagonal_hit = slash_hit[jnp.clip(distance, 0, total_blocks - 1)]
    active = (distance >= 0) & (near | vertical[None, :] | diagonal_hit)
    return active.reshape(N_COL, QBP, N_ROW, KBP)


def draw_block_count(key, part):
    return jnp.sum(active_blocks(key).astype(jnp.int32), axis=-1).astype(jnp.int32)


def draw_block_list(key, part):
    active = active_blocks(key).astype(jnp.int32)
    order_key = (1 - active) * KBP + jnp.arange(KBP, dtype=jnp.int32)
    return jnp.argsort(order_key, axis=-1, stable=True).astype(jnp.int32)


def drawn_pattern(key):
    return jax.random.bernoulli(jax.random.fold_in(key, 23), 0.5, (HD,)).astype(jnp.float32) * 2.0 - 1.0


def half_columns():
    return jnp.arange(HD, dtype=jnp.int32) < HD // 2


def far_positions():
    return (3 * SEQ // 8 + 7, 7 * SEQ // 8 + 7)


def draw_queries(key, part):
    base_key = jax.random.fold_in(key, 5)
    pattern = drawn_pattern(key)
    flat = jax.random.normal(base_key, (SEQ, GROUP * HD), jnp.float32)
    chosen_cols = half_columns()
    for position in far_positions():
        flat = flat.at[position, :HD].set(jnp.where(chosen_cols, 6.0 * pattern, flat[position, :HD]))
    flat = jnp.clip(flat, -6.0, 6.0)
    return flat.reshape(N_COL, QP, GROUP * HD).astype(jnp.bfloat16)


def draw_keys(key, part):
    base_key = jax.random.fold_in(key, 6)
    pattern = drawn_pattern(key)
    flat = jax.random.normal(base_key, (SEQ, HD), jnp.float32)
    chosen_cols = half_columns()
    sink_scale = 4.0
    sink_shrink = 2.0 * HD ** 0.5 / (6.0 * sink_scale * (HD // 2))
    flat = flat.at[0].set(jnp.where(chosen_cols, sink_scale * pattern, flat[0]))
    flat = flat.at[1].set(jnp.where(chosen_cols, sink_scale * (1.0 - sink_shrink) * pattern, flat[1]))
    flat = jnp.clip(flat, -6.0, 6.0)
    return flat.reshape(N_ROW, KP, HD).astype(jnp.bfloat16)


def block_levels(stream_key, extent, pieces, least, largest):
    factor_of = 1.0
    for dim, blocks in pieces:
        steps = jax.random.uniform(jax.random.fold_in(jax.random.fold_in(stream_key, 6), dim), (blocks,), jnp.float32, least / len(pieces), largest / len(pieces))
        factor_of = factor_of * jnp.repeat(jnp.exp(steps), extent[dim] // blocks).reshape((-1,) + (1,) * (len(extent) - 1 - dim))
    return factor_of


def centred(stream_key, dims, scale, reach, shards=(), held_as=jnp.bfloat16):
    gain = block_levels(stream_key, dims, shards, -0.22, 0.18) if shards else 1.0
    values = jax.random.normal(stream_key, dims, jnp.float32) * scale * gain
    return jnp.minimum(jnp.maximum(values, -reach), reach).astype(held_as)


def setup_inputs(seed: int = 0, part: int = 0) -> dict:
    key_list = jax.random.split(jax.random.key(seed), 6)
    part_keys = jax.random.split(jax.random.fold_in(key_list[5], part), 6)
    queries = draw_queries(jax.random.fold_in(jax.random.fold_in(key_list[5], part), 71), part)
    keys = draw_keys(jax.random.fold_in(jax.random.fold_in(key_list[5], part), 71), part)
    values = centred(part_keys[2], (N_ROW, KP, HD), 1.0, 6.0, ((0, 4), (1, 4)))
    block_list = draw_block_list(jax.random.fold_in(jax.random.fold_in(key_list[5], part), 71), part)
    block_count = draw_block_count(jax.random.fold_in(jax.random.fold_in(key_list[5], part), 71), part)
    return dict(queries=queries, keys=keys, values=values, block_list=block_list, block_count=block_count)


floor_score = -1.0e30


def attend_tile(query_blocks, slot_lists, slot_counts, first_block, key_blocks, value_blocks, key_start):
    number = query_blocks.shape[0]
    block_rows = query_blocks.shape[1]
    heads = query_blocks.shape[2]
    head_size = query_blocks.shape[3]
    query_pos = (first_block * block_rows + jnp.arange(number * block_rows, dtype=jnp.int32)).reshape(number, block_rows)
    offsets = jnp.arange(block_rows, dtype=jnp.int32)
    score_scale = 1.0 / (head_size ** 0.5)
    query_wide = query_blocks.astype(jnp.float32)
    start_state = (jnp.full((number, block_rows, heads), floor_score, jnp.float32),
                   jnp.zeros((number, block_rows, heads), jnp.float32),
                   jnp.zeros((number, block_rows, heads, head_size), jnp.float32))

    def advance(slot_index, state):
        run_max, run_sum, run_acc = state
        chosen = lax.dynamic_index_in_dim(slot_lists, slot_index, 1, keepdims=False).astype(jnp.int32)
        keys_now = jnp.take(key_blocks, chosen, axis=0).astype(jnp.float32)
        values_now = jnp.take(value_blocks, chosen, axis=0).astype(jnp.float32)
        scores = jnp.einsum("nqgd,nkd->nqgk", query_wide, keys_now, precision=lax.Precision.HIGHEST) * score_scale
        key_pos = key_start + chosen[:, None] * block_rows + offsets[None, :]
        usable = (slot_index < slot_counts)[:, None, None, None] & (query_pos[:, :, None, None] >= key_pos[:, None, None, :])
        scores = jnp.where(usable, scores, floor_score)
        new_max = jnp.maximum(run_max, jnp.max(scores, axis=-1))
        decay = jnp.exp(run_max - new_max)
        weights = jnp.where(usable, jnp.exp(scores - new_max[..., None]), 0.0)
        run_sum = run_sum * decay + jnp.sum(weights, axis=-1)
        rounded = lax.optimization_barrier(weights.astype(jnp.bfloat16)).astype(jnp.float32)
        mixed = jnp.einsum("nqgk,nkd->nqgd", rounded, values_now, precision=lax.Precision.HIGHEST)
        run_acc = run_acc * decay[..., None] + mixed
        return new_max, run_sum, run_acc

    bound = jnp.max(slot_counts).astype(jnp.int32)
    final_max, final_sum, final_acc = lax.fori_loop(jnp.int32(0), bound, advance, start_state)
    rows = number * block_rows
    return final_acc.reshape(rows, heads, head_size), final_max.reshape(rows, heads), final_sum.reshape(rows, heads)


def reference(queries, keys, values, block_list, block_count):
    key_grid = keys.reshape(N_ROW, KBP, BLOCK, HD)
    value_grid = values.reshape(N_ROW, KBP, BLOCK, HD)

    def one_query_panel(col_index):
        query_blocks = lax.dynamic_index_in_dim(queries, col_index, 0, keepdims=False).reshape(QBP, BLOCK, GROUP, HD)
        panel_lists = lax.dynamic_index_in_dim(block_list, col_index, 0, keepdims=False)
        panel_counts = lax.dynamic_index_in_dim(block_count, col_index, 0, keepdims=False)
        first_block = col_index * QBP

        def one_key_panel(state, panel_index):
            top, numer, denom = state
            part_acc, part_max, part_sum = attend_tile(
                query_blocks,
                lax.dynamic_index_in_dim(panel_lists, panel_index, 1, keepdims=False),
                lax.dynamic_index_in_dim(panel_counts, panel_index, 1, keepdims=False),
                first_block,
                lax.dynamic_index_in_dim(key_grid, panel_index, 0, keepdims=False),
                lax.dynamic_index_in_dim(value_grid, panel_index, 0, keepdims=False),
                panel_index * KP)
            new_top = jnp.maximum(top, part_max)
            old_weight = jnp.exp(top - new_top)
            part_weight = jnp.exp(part_max - new_top)
            numer = numer * old_weight[..., None] + part_acc * part_weight[..., None]
            denom = denom * old_weight + part_sum * part_weight
            return (new_top, numer, denom), None

        start_state = (jnp.full((QP, GROUP), floor_score, jnp.float32),
                       jnp.zeros((QP, GROUP, HD), jnp.float32),
                       jnp.zeros((QP, GROUP), jnp.float32))
        final_state, unused = lax.scan(one_key_panel, start_state, jnp.arange(N_ROW, dtype=jnp.int32))
        top, numer, denom = final_state
        return (numer / denom[..., None]).reshape(QP, GROUP * HD).astype(jnp.bfloat16)

    return lax.map(one_query_panel, jnp.arange(N_COL, dtype=jnp.int32))
```

```python
import functools

import jax
import jax.numpy as jnp
from jax import lax
from jax.experimental import pallas as pl
from jax.experimental.pallas import tpu as pltpu
from jax.sharding import PartitionSpec as P

NEG = -1e30
LOG2E = 1.4426950408889634
CORES = 2
REACH = 2


def kernel(
    n_row, n_col, q_ref, k_ref, v_ref, list_ref, count_ref, o_ref,
    kbuf, vbuf, q_stack, acc, run_max, run_sum, lists, counts, bias,
    list_sem, recv_sem, ready, send_z, send_x, send_s,
):
    n_x = n_col // CORES
    block = k_ref.shape[1]
    head = k_ref.shape[2]
    heads = q_ref.shape[2] // head
    slots = lists.shape[1]
    z = lax.axis_index("row")
    col = lax.axis_index("col")
    x = col // CORES
    k = col % CORES
    mine = col * n_row + z
    sibling = x * CORES + (1 - k)
    factor = LOG2E / head**0.5

    def wanted(j, at_z, at_col):
        return j <= at_col * n_row + at_z

    def chip_wanted(j, at_z, at_x):
        return j <= (at_x * CORES + CORES - 1) * n_row + at_z

    def line_wanted(j, at_z):
        return j <= (n_col - 1) * n_row + at_z

    def copy(j, part, sem, row, column):
        return pltpu.make_async_remote_copy(
            src_ref=(kbuf, vbuf)[part].at[j],
            dst_ref=(kbuf, vbuf)[part].at[j],
            send_sem=sem,
            recv_sem=recv_sem.at[j, part],
            device_id={"row": row, "col": column},
            device_id_type=pl.DeviceIdType.MESH,
        )

    def arrived(j, part):
        copy(j, part, send_s.at[0, 0, 0], z, sibling).wait_recv()

    def x_copy(r, other, part):
        return copy(r * n_col + col, part, send_x.at[r, other, part], z, other * CORES + k)

    def s_copy(r, cx, part):
        return copy(r * n_col + cx * CORES + k, part, send_s.at[r, cx, part], z, sibling)

    def z_copy(r, up, hop, part):
        to = z + hop if up else z - hop
        return copy(r * n_col + col, part, send_z.at[r, up, hop - 1, part], to, col)

    def fan_out(r, parts, act):
        j = r * n_col + col
        for dx in range(1, n_x):
            other = (x + dx) % n_x

            @pl.when(chip_wanted(j, z, other))
            def _():
                for part in parts:
                    act(x_copy(r, other, part))

        @pl.when(wanted(j, z, sibling))
        def _():
            for part in parts:
                act(s_copy(r, x, part))

    def onward(r, up, parts, act, hops=(1, 2)):
        for hop in hops:
            to = z + hop if up else z - hop

            @pl.when((to >= 0) & (to < n_row) & line_wanted(r * n_col + col, to))
            def _():
                for part in parts:
                    act(z_copy(r, up, hop, part))

    def both_ways(r, parts, act):
        for up in (1, 0):
            @pl.when(((r <= z) if up else (r >= z)) & ((z - r) % REACH == 0))
            def _():
                onward(r, up, parts, act)

    def start(c):
        c.start()

    def wait_send(c):
        c.wait_send()

    list_copies = (
        pltpu.make_async_copy(list_ref.at[col, z], lists, list_sem.at[0]),
        pltpu.make_async_copy(count_ref.at[col, pl.ds(z, 1)], counts, list_sem.at[1]),
    )
    own = z * n_col + col
    own_copies = (
        pltpu.make_async_copy(k_ref.at[0], kbuf.at[own], list_sem.at[2]),
        pltpu.make_async_copy(v_ref.at[0], vbuf.at[own], list_sem.at[3]),
    )
    q_copies = [
        pltpu.make_async_copy(
            q_ref.at[0, :, pl.ds(h * head, head)], q_stack.at[pl.ds(h * block, block)], list_sem.at[4 + h]
        )
        for h in range(heads)
    ]
    for c in (*own_copies, *list_copies, *q_copies):
        c.start()

    barrier = pltpu.get_barrier_semaphore()

    def greet(row, column):
        pl.semaphore_signal(
            barrier, inc=1, device_id={"row": row, "col": column}, device_id_type=pl.DeviceIdType.MESH
        )

    greeted = jnp.int32(n_x)
    for to in (z - 1, z + 1):
        inside = (to >= 0) & (to < n_row)
        greeted += jnp.where(inside, 1, 0)

        @pl.when(inside)
        def _():
            greet(to, col)

    for dx in range(1, n_x):
        greet(z, ((x + dx) % n_x) * CORES + k)
    greet(z, sibling)
    pl.semaphore_wait(barrier, greeted)

    for c in own_copies:
        c.wait()

    @pl.when((z > 0) & (z + 1 < n_row))
    def _():
        for up, to in ((1, z - 1), (0, z + 1)):
            pl.semaphore_signal(
                ready.at[up], inc=1, device_id={"row": to, "col": col},
                device_id_type=pl.DeviceIdType.MESH,
            )

    for up in (1, 0):
        onward(z, up, (0, 1), start, (1,))
    fan_out(z, (0, 1), start)
    for up, far in ((1, z + 2), (0, z - 2)):
        @pl.when((far >= 0) & (far < n_row))
        def _():
            pl.semaphore_wait(ready.at[up], 1)
            onward(z, up, (0, 1), start, (2,))

    acc[...] = jnp.zeros_like(acc)
    run_sum[...] = jnp.zeros_like(run_sum)
    run_max[...] = jnp.full_like(run_max, NEG)
    for c in (*list_copies, *q_copies):
        c.wait()

    def fill(r, carry):
        for p in range(slots):
            hit = jnp.int32(0)
            for s in range(slots):
                hit += jnp.where((lists[r, s] == p) & (s < counts[0, r]), 1, 0)
            bias[r * slots + p] = jnp.where(hit > 0, 0.0, NEG).astype(jnp.float32)
        return carry

    lax.fori_loop(0, n_row, fill, 0)

    def attend(j, count, masked):
        rows = count * block
        key = kbuf[pl.ds(j, count)].reshape(rows, head)
        value = vbuf[pl.ds(j, count)].reshape(rows, head)
        s = lax.dot_general(
            key, q_stack[...], (((1,), (1,)), ((), ())), preferred_element_type=jnp.float32
        )
        s = jnp.concatenate(
            [s[b * block : (b + 1) * block] + bias[j + b] for b in range(count)], axis=0
        )
        if masked:
            key_row = lax.broadcasted_iota(jnp.int32, s.shape, 0)
            query_row = lax.broadcasted_iota(jnp.int32, s.shape, 1) % block
            s = jnp.where(key_row - query_row <= (mine - j) * block, s, NEG)
        old = run_max[...]
        new = jnp.maximum(old, jnp.max(s, axis=0, keepdims=True))
        w = jnp.exp2((s - new) * factor)
        decay = jnp.exp2((old - new) * factor)
        run_max[...] = new
        run_sum[...] = run_sum[...] * decay + jnp.sum(w, axis=0, keepdims=True)
        acc[...] = acc[...] * decay + lax.dot_general(
            value, w.astype(jnp.bfloat16), (((0,), (0,)), ((), ())),
            preferred_element_type=jnp.float32,
        )

    def relay_line(r):
        j = r * n_col + col

        @pl.when(line_wanted(j, z))
        def _():
            for part in range(2):
                arrived(j, part)
                both_ways(r, (part,), start)
                fan_out(r, (part,), start)

    def relay_chips(r):
        for dx in range(1, n_x):
            cx = (x + dx) % n_x
            j = r * n_col + cx * CORES + k

            @pl.when(chip_wanted(j, z, x))
            def _():
                for part in range(2):
                    arrived(j, part)

                    @pl.when(wanted(j, z, sibling))
                    def _():
                        s_copy(r, cx, part).start()

    def attend_panel(r):
        for dx in range(n_x):
            first = r * n_col + ((x + dx) % n_x) * CORES
            theirs = first + 1 - k

            @pl.when(wanted(theirs, z, col))
            def _():
                for part in range(2):
                    arrived(theirs, part)

            @pl.when(first + CORES <= mine)
            def _():
                attend(first, CORES, False)

            for c in range(CORES):
                @pl.when((first + CORES > mine) & (first + c <= mine))
                def _():
                    attend(first + c, 1, True)

    def at_distance(d, act):
        for r, first in ((z - d, True), (z + d, False)):
            @pl.when((r >= 0) & (r < n_row) & (first | (d > 0)))
            def _():
                act(r)

    relay_chips(z)
    at_distance(1, relay_line)

    def step(d, carry):
        at_distance(d, relay_line)
        at_distance(d - 1, relay_chips)
        at_distance(d - 2, attend_panel)
        return carry

    lax.fori_loop(2, n_row, step, 0)
    at_distance(n_row - 1, relay_chips)
    at_distance(n_row - 2, attend_panel)
    at_distance(n_row - 1, attend_panel)

    for h in range(heads):
        part = slice(h * block, (h + 1) * block)
        o_ref[0, :, h * head : (h + 1) * head] = (
            (acc[:, part] / run_sum[:, part]).T.astype(o_ref.dtype)
        )

    both_ways(z, (0, 1), wait_send)
    fan_out(z, (0, 1), wait_send)

    def drain(r, carry):
        @pl.when((r != z) & line_wanted(r * n_col + col, z))
        def _():
            both_ways(r, (0, 1), wait_send)
            fan_out(r, (0, 1), wait_send)

        for dx in range(1, n_x):
            cx = (x + dx) % n_x
            j = r * n_col + cx * CORES + k

            @pl.when(wanted(j, z, sibling))
            def _():
                for part in range(2):
                    s_copy(r, cx, part).wait_send()

        return carry

    lax.fori_loop(0, n_row, drain, 0)


def per_device(n_row, n_col, queries, keys, values, block_list, block_count):
    block, head = keys.shape[1], keys.shape[2]
    wide = queries.shape[1] * (queries.shape[2] // head)
    slots = block_list.shape[3]
    assert queries.shape[1] == block and slots == n_col and block_list.shape[1] == n_row
    blocks = n_row * n_col
    vmem = pl.BlockSpec(memory_space=pltpu.VMEM)
    hbm = pl.BlockSpec(memory_space=pl.ANY)
    return pl.pallas_call(
        functools.partial(kernel, n_row, n_col),
        out_shape=pltpu.VMEM(queries.shape, queries.dtype),
        in_specs=[hbm] * 5,
        out_specs=vmem,
        scratch_shapes=[
            pltpu.VMEM((blocks, block, head), keys.dtype),
            pltpu.VMEM((blocks, block, head), values.dtype),
            pltpu.VMEM((wide, head), queries.dtype),
            pltpu.VMEM((head, wide), jnp.float32),
            pltpu.VMEM((1, wide), jnp.float32),
            pltpu.VMEM((1, wide), jnp.float32),
            pltpu.SMEM((n_row, slots), jnp.int32),
            pltpu.SMEM((1, n_row), jnp.int32),
            pltpu.SMEM((blocks,), jnp.float32),
            pltpu.SemaphoreType.DMA((4 + wide // block,)),
            pltpu.SemaphoreType.DMA((blocks, 2)),
            pltpu.SemaphoreType.REGULAR((2,)),
            pltpu.SemaphoreType.DMA((n_row, 2, REACH, 2)),
            pltpu.SemaphoreType.DMA((n_row, n_col // CORES, 2)),
            pltpu.SemaphoreType.DMA((n_row, n_col // CORES, 2)),
        ],
        compiler_params=pltpu.CompilerParams(collective_id=0, has_side_effects=True),
        name="gather_attend",
    )(*(pltpu.with_memory_space_constraint(a, pltpu.HBM) for a in (queries, keys, values, block_list, block_count)))


def solution(mesh):
    placed = (
        P(("groups", "col"), "row", None),
        P(("groups", "row"), "col", None),
        P(("groups", "row"), "col", None),
        P("groups", None, None, None),
        P("groups", None, None),
    )
    return jax.shard_map(
        functools.partial(per_device, mesh.shape["row"], mesh.shape["col"]),
        mesh=mesh,
        in_specs=placed,
        out_specs=P(("groups", "col"), "row", None),
        check_vma=False,
    )
```

```python
import functools

import jax
import jax.numpy as jnp
from jax import lax
from jax.experimental import pallas as pl
from jax.experimental.pallas import tpu as pltpu
from jax.sharding import PartitionSpec as P

NEG = -1e30
LOG2E = 1.4426950408889634
CORES = 2
REACH = 3
HOPS = (1, REACH)


def kernel(
    n_row, n_col, q_ref, k_ref, v_ref, list_ref, count_ref, o_ref,
    kbuf, vbuf, q_stack, acc, run_max, run_sum, lists, counts, bias,
    list_sem, recv_sem, ready_z, ready_x, send_z, send_x, send_s,
):
    n_x = n_col // CORES
    block = k_ref.shape[1]
    head = k_ref.shape[2]
    heads = q_ref.shape[2] // head
    slots = lists.shape[1]
    z = lax.axis_index("row")
    col = lax.axis_index("col")
    x = col // CORES
    k = col % CORES
    mine = col * n_row + z
    sibling = x * CORES + (1 - k)
    factor = LOG2E / head**0.5

    def wanted(j, at_z, at_col):
        return j <= at_col * n_row + at_z

    def chip_wanted(j, at_z, at_x):
        return j <= (at_x * CORES + CORES - 1) * n_row + at_z

    def line_wanted(j, at_z):
        return j <= (n_col - 1) * n_row + at_z

    def copy(j, part, sem, row, column):
        return pltpu.make_async_remote_copy(
            src_ref=(kbuf, vbuf)[part].at[j],
            dst_ref=(kbuf, vbuf)[part].at[j],
            send_sem=sem,
            recv_sem=recv_sem.at[j, part],
            device_id={"row": row, "col": column},
            device_id_type=pl.DeviceIdType.MESH,
        )

    def arrived(j, part):
        copy(j, part, send_s.at[0, 0, 0], z, sibling).wait_recv()

    def x_copy(r, other, part):
        j = r * n_col + col
        same = other * CORES + k
        to = jnp.where(wanted(j, z, same), same, other * CORES + CORES - 1)
        return copy(j, part, send_x.at[r, other, part], z, to)

    def s_copy(r, cx, part):
        return copy(r * n_col + cx * CORES + k, part, send_s.at[r, cx, part], z, sibling)

    def z_copy(r, up, hop, part):
        to = z + hop if up else z - hop
        return copy(r * n_col + col, part, send_z.at[r, up, int(hop > 1), part], to, col)

    def to_chips(r, parts, act, higher):
        j = r * n_col + col
        for dx in range(1, n_x):
            other = x + dx if higher else x - dx

            @pl.when(((other < n_x) if higher else (other >= 0)) & chip_wanted(j, z, other))
            def _():
                for part in parts:
                    act(x_copy(r, other, part))

    def to_sibling(r, parts, act):
        @pl.when(wanted(r * n_col + col, z, sibling))
        def _():
            for part in parts:
                act(s_copy(r, x, part))

    def fan_out(r, parts, act):
        for higher in (True, False):
            to_chips(r, parts, act, higher)
        to_sibling(r, parts, act)

    def onward(r, up, parts, act, hops=HOPS):
        for hop in hops:
            to = z + hop if up else z - hop
            gone = (z - r if up else r - z) % REACH

            @pl.when(
                (gone < (2 if hop == 1 else 1)) & (to >= 0) & (to < n_row)
                & line_wanted(r * n_col + col, to)
            )
            def _():
                for part in parts:
                    act(z_copy(r, up, hop, part))

    def both_ways(r, parts, act):
        for up in (1, 0):
            @pl.when((r <= z) if up else (r >= z))
            def _():
                onward(r, up, parts, act)

    def start(c):
        c.start()

    def wait_send(c):
        c.wait_send()

    list_copies = (
        pltpu.make_async_copy(list_ref.at[col, z], lists, list_sem.at[0]),
        pltpu.make_async_copy(count_ref.at[col, pl.ds(z, 1)], counts, list_sem.at[1]),
    )
    own = z * n_col + col
    own_copies = (
        pltpu.make_async_copy(k_ref.at[0], kbuf.at[own], list_sem.at[2]),
        pltpu.make_async_copy(v_ref.at[0], vbuf.at[own], list_sem.at[3]),
    )
    q_copies = [
        pltpu.make_async_copy(
            q_ref.at[0, :, pl.ds(h * head, head)], q_stack.at[pl.ds(h * block, block)], list_sem.at[4 + h]
        )
        for h in range(heads)
    ]
    for c in (*own_copies, *list_copies, *q_copies):
        c.start()

    barrier = pltpu.get_barrier_semaphore()

    def signal(sem, row, column):
        pl.semaphore_signal(
            sem, inc=1, device_id={"row": row, "col": column}, device_id_type=pl.DeviceIdType.MESH
        )

    greeted = x * CORES + 1
    for hop in HOPS:
        greeted += jnp.where(z >= hop, 1, 0)

        @pl.when(z + hop < n_row)
        def _():
            signal(barrier, z + hop, col)

    for dx in range(1, n_x):
        @pl.when(x + dx < n_x)
        def _():
            for c in range(CORES):
                signal(barrier, z, (x + dx) * CORES + c)

    signal(barrier, z, sibling)
    pl.semaphore_wait(barrier, greeted)

    for hop in HOPS:
        @pl.when(z >= hop)
        def _():
            signal(ready_z.at[int(hop > 1)], z - hop, col)

    for dx in range(1, n_x):
        @pl.when(x >= dx)
        def _():
            for c in range(CORES):
                signal(ready_x.at[dx - 1], z, (x - dx) * CORES + c)

    for c in own_copies:
        c.wait()

    onward(z, 0, (0, 1), start)
    to_chips(z, (0, 1), start, False)
    to_sibling(z, (0, 1), start)
    for hop in HOPS:
        @pl.when(z + hop < n_row)
        def _():
            pl.semaphore_wait(ready_z.at[int(hop > 1)], 1)
            onward(z, 1, (0, 1), start, (hop,))

        if hop == 1:
            for dx in range(1, n_x):
                @pl.when(x + dx < n_x)
                def _():
                    pl.semaphore_wait(ready_x.at[dx - 1], CORES)

            to_chips(z, (0, 1), start, True)

    acc[...] = jnp.zeros_like(acc)
    run_sum[...] = jnp.zeros_like(run_sum)
    run_max[...] = jnp.full_like(run_max, NEG)
    for c in (*list_copies, *q_copies):
        c.wait()

    def fill(r, carry):
        for p in range(slots):
            hit = jnp.int32(0)
            for s in range(slots):
                hit += jnp.where((lists[r, s] == p) & (s < counts[0, r]), 1, 0)
            bias[r * slots + p] = jnp.where(hit > 0, 0.0, NEG).astype(jnp.float32)
        return carry

    lax.fori_loop(0, n_row, fill, 0)

    def attend(j, count, masked):
        rows = count * block
        key = kbuf[pl.ds(j, count)].reshape(rows, head)
        value = vbuf[pl.ds(j, count)].reshape(rows, head)
        s = lax.dot_general(
            key, q_stack[...], (((1,), (1,)), ((), ())), preferred_element_type=jnp.float32
        )
        s = jnp.concatenate(
            [s[b * block : (b + 1) * block] + bias[j + b] for b in range(count)], axis=0
        )
        if masked:
            key_row = lax.broadcasted_iota(jnp.int32, s.shape, 0)
            query_row = lax.broadcasted_iota(jnp.int32, s.shape, 1) % block
            s = jnp.where(key_row - query_row <= (mine - j) * block, s, NEG)
        old = run_max[...]
        new = jnp.maximum(old, jnp.max(s, axis=0, keepdims=True))
        w = jnp.exp2((s - new) * factor)
        decay = jnp.exp2((old - new) * factor)
        run_max[...] = new
        run_sum[...] = run_sum[...] * decay + jnp.sum(w, axis=0, keepdims=True)
        acc[...] = acc[...] * decay + lax.dot_general(
            value, w.astype(jnp.bfloat16), (((0,), (0,)), ((), ())),
            preferred_element_type=jnp.float32,
        )

    def relay_line(r):
        j = r * n_col + col

        @pl.when(line_wanted(j, z))
        def _():
            for part in range(2):
                arrived(j, part)
                both_ways(r, (part,), start)
                fan_out(r, (part,), start)

    def relay_chips(r):
        for dx in range(1, n_x):
            cx = (x + dx) % n_x
            j = r * n_col + cx * CORES + k
            theirs = r * n_col + cx * CORES + 1 - k

            @pl.when(wanted(j, z, col))
            def _():
                for part in range(2):
                    arrived(j, part)

                    @pl.when(wanted(j, z, sibling))
                    def _():
                        s_copy(r, cx, part).start()

            @pl.when(wanted(theirs, z, col) & jnp.logical_not(wanted(theirs, z, sibling)))
            def _():
                for part in range(2):
                    arrived(theirs, part)

    def attend_chips(r, dxs):
        for dx in dxs:
            first = r * n_col + ((x + dx) % n_x) * CORES
            theirs = first + 1 - k
            passed = wanted(theirs, z, col)
            if dx:
                passed &= wanted(theirs, z, sibling)

            @pl.when(passed)
            def _():
                for part in range(2):
                    arrived(theirs, part)

            @pl.when(first + CORES <= mine)
            def _():
                attend(first, CORES, False)

            for c in range(CORES):
                @pl.when((first + CORES > mine) & (first + c <= mine))
                def _():
                    attend(first + c, 1, True)

    def at_distance(d, act):
        for r, first in ((z - d, True), (z + d, False)):
            @pl.when((r >= 0) & (r < n_row) & (first | (d > 0)))
            def _():
                act(r)

    def near(t, act):
        d = t + jnp.where(t % REACH == 2, 1, 0) - jnp.where((t % REACH == 0) & (t > 0), 1, 0)
        at_distance(d, act)

    def attend_near(r):
        attend_chips(r, (0,))

    def attend_far(r):
        attend_chips(r, range(1, n_x))

    at_distance(1, relay_line)
    relay_chips(z)
    near(jnp.int32(2), relay_line)
    attend_near(z)

    def step(t, carry):
        near(t, attend_far)
        near(t + 3, relay_line)
        near(t + 1, relay_chips)
        near(t + 1, attend_near)
        return carry

    lax.fori_loop(0, 1 - (1 - n_row) // REACH * REACH, step, 0)

    for h in range(heads):
        part = slice(h * block, (h + 1) * block)
        o_ref[0, :, h * head : (h + 1) * head] = (
            (acc[:, part] / run_sum[:, part]).T.astype(o_ref.dtype)
        )

    both_ways(z, (0, 1), wait_send)
    fan_out(z, (0, 1), wait_send)

    def drain(r, carry):
        @pl.when((r != z) & line_wanted(r * n_col + col, z))
        def _():
            both_ways(r, (0, 1), wait_send)
            fan_out(r, (0, 1), wait_send)

        for dx in range(1, n_x):
            cx = (x + dx) % n_x
            j = r * n_col + cx * CORES + k

            @pl.when(wanted(j, z, sibling) & wanted(j, z, col))
            def _():
                for part in range(2):
                    s_copy(r, cx, part).wait_send()

        return carry

    lax.fori_loop(0, n_row, drain, 0)


def per_device(n_row, n_col, queries, keys, values, block_list, block_count):
    block, head = keys.shape[1], keys.shape[2]
    wide = queries.shape[1] * (queries.shape[2] // head)
    slots = block_list.shape[3]
    assert queries.shape[1] == block and slots == n_col and block_list.shape[1] == n_row
    blocks = n_row * n_col
    vmem = pl.BlockSpec(memory_space=pltpu.VMEM)
    hbm = pl.BlockSpec(memory_space=pl.ANY)
    return pl.pallas_call(
        functools.partial(kernel, n_row, n_col),
        out_shape=pltpu.VMEM(queries.shape, queries.dtype),
        in_specs=[hbm] * 5,
        out_specs=vmem,
        scratch_shapes=[
            pltpu.VMEM((blocks, block, head), keys.dtype),
            pltpu.VMEM((blocks, block, head), values.dtype),
            pltpu.VMEM((wide, head), queries.dtype),
            pltpu.VMEM((head, wide), jnp.float32),
            pltpu.VMEM((1, wide), jnp.float32),
            pltpu.VMEM((1, wide), jnp.float32),
            pltpu.SMEM((n_row, slots), jnp.int32),
            pltpu.SMEM((1, n_row), jnp.int32),
            pltpu.SMEM((blocks,), jnp.float32),
            pltpu.SemaphoreType.DMA((4 + wide // block,)),
            pltpu.SemaphoreType.DMA((blocks, 2)),
            pltpu.SemaphoreType.REGULAR((len(HOPS),)),
            pltpu.SemaphoreType.REGULAR((max(1, n_col // CORES - 1),)),
            pltpu.SemaphoreType.DMA((n_row, 2, len(HOPS), 2)),
            pltpu.SemaphoreType.DMA((n_row, n_col // CORES, 2)),
            pltpu.SemaphoreType.DMA((n_row, n_col // CORES, 2)),
        ],
        compiler_params=pltpu.CompilerParams(collective_id=0, has_side_effects=True),
        name="gather_attend",
    )(*(pltpu.with_memory_space_constraint(a, pltpu.HBM) for a in (queries, keys, values, block_list, block_count)))


def solution(mesh):
    placed = (
        P(("groups", "col"), "row", None),
        P(("groups", "row"), "col", None),
        P(("groups", "row"), "col", None),
        P("groups", None, None, None),
        P("groups", None, None),
    )
    return jax.shard_map(
        functools.partial(per_device, mesh.shape["row"], mesh.shape["col"]),
        mesh=mesh,
        in_specs=placed,
        out_specs=P(("groups", "col"), "row", None),
        check_vma=False,
    )
```

```python
import functools

import jax
import jax.numpy as jnp
from jax import lax
from jax.experimental import pallas as pl
from jax.experimental.pallas import tpu as pltpu
from jax.sharding import PartitionSpec as P

NEG = -1e30
LOG2E = 1.4426950408889634
CORES = 2
REACH = 3
HOPS = (1, REACH)


def kernel(
    n_row, n_col, q_ref, k_ref, v_ref, list_ref, count_ref, o_ref,
    kbuf, vbuf, q_stack, acc, run_max, run_sum, lists, counts, bias,
    list_sem, recv_sem, ready_z, ready_x, send_z, send_x, send_s,
):
    n_x = n_col // CORES
    block = k_ref.shape[1]
    head = k_ref.shape[2]
    heads = q_ref.shape[2] // head
    slots = lists.shape[1]
    z = lax.axis_index("row")
    col = lax.axis_index("col")
    x = col // CORES
    k = col % CORES
    mine = col * n_row + z
    sibling = x * CORES + (1 - k)
    factor = LOG2E / head**0.5

    def wanted(j, at_z, at_col):
        return j <= at_col * n_row + at_z

    def chip_wanted(j, at_z, at_x):
        return j <= (at_x * CORES + CORES - 1) * n_row + at_z

    def line_wanted(j, at_z):
        return j <= (n_col - 1) * n_row + at_z

    def copy(j, part, sem, row, column):
        return pltpu.make_async_remote_copy(
            src_ref=(kbuf, vbuf)[part].at[j],
            dst_ref=(kbuf, vbuf)[part].at[j],
            send_sem=sem,
            recv_sem=recv_sem.at[j, part],
            device_id={"row": row, "col": column},
            device_id_type=pl.DeviceIdType.MESH,
        )

    def arrived(j, part):
        copy(j, part, send_s.at[0, 0, 0], z, sibling).wait_recv()

    def x_copy(r, other, part):
        j = r * n_col + col
        same = other * CORES + k
        to = jnp.where(wanted(j, z, same), same, other * CORES + CORES - 1)
        return copy(j, part, send_x.at[r, other, part], z, to)

    def s_copy(r, cx, part):
        return copy(r * n_col + cx * CORES + k, part, send_s.at[r, cx, part], z, sibling)

    def z_copy(r, up, hop, part):
        to = z + hop if up else z - hop
        return copy(r * n_col + col, part, send_z.at[r, up, int(hop > 1), part], to, col)

    def to_chips(r, parts, act, higher):
        j = r * n_col + col
        for dx in range(1, n_x):
            other = x + dx if higher else x - dx

            @pl.when(((other < n_x) if higher else (other >= 0)) & chip_wanted(j, z, other))
            def _():
                for part in parts:
                    act(x_copy(r, other, part))

    def to_sibling(r, parts, act):
        @pl.when(wanted(r * n_col + col, z, sibling))
        def _():
            for part in parts:
                act(s_copy(r, x, part))

    def fan_out(r, parts, act):
        for higher in (True, False):
            to_chips(r, parts, act, higher)
        to_sibling(r, parts, act)

    def onward(r, up, parts, act, hops=HOPS):
        for hop in hops:
            to = z + hop if up else z - hop
            gone = (z - r if up else r - z) % REACH

            @pl.when(
                (gone < (2 if hop == 1 else 1)) & (to >= 0) & (to < n_row)
                & line_wanted(r * n_col + col, to)
            )
            def _():
                for part in parts:
                    act(z_copy(r, up, hop, part))

    def both_ways(r, parts, act):
        for up in (1, 0):
            @pl.when((r <= z) if up else (r >= z))
            def _():
                onward(r, up, parts, act)

    def start(c):
        c.start()

    def wait_send(c):
        c.wait_send()

    list_copies = (
        pltpu.make_async_copy(list_ref.at[col, z], lists, list_sem.at[0]),
        pltpu.make_async_copy(count_ref.at[col, pl.ds(z, 1)], counts, list_sem.at[1]),
    )
    own = z * n_col + col
    own_copies = (
        pltpu.make_async_copy(k_ref.at[0], kbuf.at[own], list_sem.at[2]),
        pltpu.make_async_copy(v_ref.at[0], vbuf.at[own], list_sem.at[3]),
    )
    q_copies = [
        pltpu.make_async_copy(
            q_ref.at[0, :, pl.ds(h * head, head)], q_stack.at[pl.ds(h * block, block)], list_sem.at[4 + h]
        )
        for h in range(heads)
    ]
    for c in (*own_copies, *list_copies, *q_copies):
        c.start()

    barrier = pltpu.get_barrier_semaphore()

    def signal(sem, row, column):
        pl.semaphore_signal(
            sem, inc=1, device_id={"row": row, "col": column}, device_id_type=pl.DeviceIdType.MESH
        )

    greeted = x * CORES + 1
    for hop in HOPS:
        greeted += jnp.where(z >= hop, 1, 0)

        @pl.when(z + hop < n_row)
        def _():
            signal(barrier, z + hop, col)

    for dx in range(1, n_x):
        @pl.when(x + dx < n_x)
        def _():
            for c in range(CORES):
                signal(barrier, z, (x + dx) * CORES + c)

    signal(barrier, z, sibling)
    pl.semaphore_wait(barrier, greeted)

    for hop in HOPS:
        @pl.when(z >= hop)
        def _():
            signal(ready_z.at[int(hop > 1)], z - hop, col)

    for dx in range(1, n_x):
        @pl.when(x >= dx)
        def _():
            for c in range(CORES):
                signal(ready_x.at[dx - 1], z, (x - dx) * CORES + c)

    for c in own_copies:
        c.wait()

    onward(z, 0, (0, 1), start)
    to_chips(z, (0, 1), start, False)
    to_sibling(z, (0, 1), start)
    for hop in HOPS:
        @pl.when(z + hop < n_row)
        def _():
            pl.semaphore_wait(ready_z.at[int(hop > 1)], 1)
            onward(z, 1, (0, 1), start, (hop,))

        if hop == 1:
            for dx in range(1, n_x):
                @pl.when(x + dx < n_x)
                def _():
                    pl.semaphore_wait(ready_x.at[dx - 1], CORES)

            to_chips(z, (0, 1), start, True)

    acc[...] = jnp.zeros_like(acc)
    run_sum[...] = jnp.zeros_like(run_sum)
    run_max[...] = jnp.full_like(run_max, NEG)
    for c in (*list_copies, *q_copies):
        c.wait()

    def fill(r, carry):
        for p in range(slots):
            hit = jnp.int32(0)
            for s in range(slots):
                hit += jnp.where((lists[r, s] == p) & (s < counts[0, r]), 1, 0)
            bias[r * slots + p] = jnp.where(hit > 0, 0.0, NEG).astype(jnp.float32)
        return carry

    lax.fori_loop(0, n_row, fill, 0)

    def attend(j, count, masked):
        rows = count * block
        key = kbuf[pl.ds(j, count)].reshape(rows, head)
        value = vbuf[pl.ds(j, count)].reshape(rows, head)
        s = lax.dot_general(
            key, q_stack[...], (((1,), (1,)), ((), ())), preferred_element_type=jnp.float32
        )
        s = jnp.concatenate(
            [s[b * block : (b + 1) * block] + bias[j + b] for b in range(count)], axis=0
        )
        if masked:
            key_row = lax.broadcasted_iota(jnp.int32, s.shape, 0)
            query_row = lax.broadcasted_iota(jnp.int32, s.shape, 1) % block
            s = jnp.where(key_row - query_row <= (mine - j) * block, s, NEG)
        old = run_max[...]
        new = jnp.maximum(old, jnp.max(s, axis=0, keepdims=True))
        w = jnp.exp2((s - new) * factor)
        decay = jnp.exp2((old - new) * factor)
        run_max[...] = new
        run_sum[...] = run_sum[...] * decay + jnp.sum(w, axis=0, keepdims=True)
        acc[...] = acc[...] * decay + lax.dot_general(
            value, w.astype(jnp.bfloat16), (((0,), (0,)), ((), ())),
            preferred_element_type=jnp.float32,
        )

    def relay_line(r):
        j = r * n_col + col

        @pl.when(line_wanted(j, z))
        def _():
            for part in range(2):
                arrived(j, part)
                both_ways(r, (part,), start)
                fan_out(r, (part,), start)

    def relay_chips(r):
        for dx in range(1, n_x):
            cx = (x + dx) % n_x
            j = r * n_col + cx * CORES + k
            theirs = r * n_col + cx * CORES + 1 - k

            @pl.when(wanted(j, z, col))
            def _():
                for part in range(2):
                    arrived(j, part)

                    @pl.when(wanted(j, z, sibling))
                    def _():
                        s_copy(r, cx, part).start()

            @pl.when(wanted(theirs, z, col) & jnp.logical_not(wanted(theirs, z, sibling)))
            def _():
                for part in range(2):
                    arrived(theirs, part)

    def attend_chips(r, dxs):
        for dx in dxs:
            first = r * n_col + ((x + dx) % n_x) * CORES
            theirs = first + 1 - k
            passed = wanted(theirs, z, col)
            if dx:
                passed &= wanted(theirs, z, sibling)

            @pl.when(passed)
            def _():
                for part in range(2):
                    arrived(theirs, part)

            @pl.when(first + CORES <= mine)
            def _():
                attend(first, CORES, False)

            for c in range(CORES):
                @pl.when(first + c == mine)
                def _():
                    attend(first, c + 1, True)

    def at_distance(d, act):
        for r, first in ((z - d, True), (z + d, False)):
            @pl.when((r >= 0) & (r < n_row) & (first | (d > 0)))
            def _():
                act(r)

    def near(t, act):
        d = t + jnp.where(t % REACH == 2, 1, 0) - jnp.where((t % REACH == 0) & (t > 0), 1, 0)
        at_distance(d, act)

    def attend_near(r):
        attend_chips(r, (0,))

    def attend_far(r):
        attend_chips(r, range(1, n_x))

    at_distance(1, relay_line)
    relay_chips(z)
    near(jnp.int32(2), relay_line)
    attend_near(z)

    def step(t, carry):
        near(t + 3, relay_line)
        near(t + 1, attend_near)
        near(t + 1, relay_chips)
        near(t + 0, attend_far)
        return carry

    lax.fori_loop(0, 1 - (1 - n_row) // REACH * REACH, step, 0)

    for h in range(heads):
        part = slice(h * block, (h + 1) * block)
        o_ref[0, :, h * head : (h + 1) * head] = (
            (acc[:, part] / run_sum[:, part]).T.astype(o_ref.dtype)
        )

    both_ways(z, (0, 1), wait_send)
    fan_out(z, (0, 1), wait_send)

    def drain(r, carry):
        @pl.when((r != z) & line_wanted(r * n_col + col, z))
        def _():
            both_ways(r, (0, 1), wait_send)
            fan_out(r, (0, 1), wait_send)

        for dx in range(1, n_x):
            cx = (x + dx) % n_x
            j = r * n_col + cx * CORES + k

            @pl.when(wanted(j, z, sibling) & wanted(j, z, col))
            def _():
                for part in range(2):
                    s_copy(r, cx, part).wait_send()

        return carry

    lax.fori_loop(0, n_row, drain, 0)


def per_device(n_row, n_col, queries, keys, values, block_list, block_count):
    block, head = keys.shape[1], keys.shape[2]
    wide = queries.shape[1] * (queries.shape[2] // head)
    slots = block_list.shape[3]
    assert queries.shape[1] == block and slots == n_col and block_list.shape[1] == n_row
    blocks = n_row * n_col
    vmem = pl.BlockSpec(memory_space=pltpu.VMEM)
    hbm = pl.BlockSpec(memory_space=pl.ANY)
    return pl.pallas_call(
        functools.partial(kernel, n_row, n_col),
        out_shape=pltpu.VMEM(queries.shape, queries.dtype),
        in_specs=[hbm] * 5,
        out_specs=vmem,
        scratch_shapes=[
            pltpu.VMEM((blocks, block, head), keys.dtype),
            pltpu.VMEM((blocks, block, head), values.dtype),
            pltpu.VMEM((wide, head), queries.dtype),
            pltpu.VMEM((head, wide), jnp.float32),
            pltpu.VMEM((1, wide), jnp.float32),
            pltpu.VMEM((1, wide), jnp.float32),
            pltpu.SMEM((n_row, slots), jnp.int32),
            pltpu.SMEM((1, n_row), jnp.int32),
            pltpu.SMEM((blocks,), jnp.float32),
            pltpu.SemaphoreType.DMA((4 + wide // block,)),
            pltpu.SemaphoreType.DMA((blocks, 2)),
            pltpu.SemaphoreType.REGULAR((len(HOPS),)),
            pltpu.SemaphoreType.REGULAR((max(1, n_col // CORES - 1),)),
            pltpu.SemaphoreType.DMA((n_row, 2, len(HOPS), 2)),
            pltpu.SemaphoreType.DMA((n_row, n_col // CORES, 2)),
            pltpu.SemaphoreType.DMA((n_row, n_col // CORES, 2)),
        ],
        compiler_params=pltpu.CompilerParams(collective_id=0, has_side_effects=True),
        name="gather_attend",
    )(*(pltpu.with_memory_space_constraint(a, pltpu.HBM) for a in (queries, keys, values, block_list, block_count)))


def solution(mesh):
    placed = (
        P(("groups", "col"), "row", None),
        P(("groups", "row"), "col", None),
        P(("groups", "row"), "col", None),
        P("groups", None, None, None),
        P("groups", None, None),
    )
    return jax.shard_map(
        functools.partial(per_device, mesh.shape["row"], mesh.shape["col"]),
        mesh=mesh,
        in_specs=placed,
        out_specs=P(("groups", "col"), "row", None),
        check_vma=False,
    )
```

```python
import functools

import jax
import jax.numpy as jnp
from jax import lax
from jax.experimental import pallas as pl
from jax.experimental.pallas import tpu as pltpu
from jax.sharding import PartitionSpec as P

NEG = -1e30
LOG2E = 1.4426950408889634
CORES = 2
REACH = 3
UP = (1, REACH)
DOWN = (3, 1, 2)


def kernel(
    n_row, n_col, q_ref, k_ref, v_ref, list_ref, count_ref, o_ref,
    kbuf, vbuf, q_stack, acc, run_max, run_sum, lists, counts, bias,
    list_sem, recv_sem, ready_z, ready_x, send_z, send_x, send_s,
):
    n_x = n_col // CORES
    block = k_ref.shape[1]
    head = k_ref.shape[2]
    heads = q_ref.shape[2] // head
    slots = lists.shape[1]
    z = lax.axis_index("row")
    col = lax.axis_index("col")
    x = col // CORES
    k = col % CORES
    mine = col * n_row + z
    sibling = x * CORES + (1 - k)
    factor = LOG2E / head**0.5

    def wanted(j, at_z, at_col):
        return j <= at_col * n_row + at_z

    def chip_wanted(j, at_z, at_x):
        return j <= (at_x * CORES + CORES - 1) * n_row + at_z

    def line_wanted(j, at_z):
        return j <= (n_col - 1) * n_row + at_z

    def copy(j, part, sem, row, column):
        return pltpu.make_async_remote_copy(
            src_ref=(kbuf, vbuf)[part].at[j],
            dst_ref=(kbuf, vbuf)[part].at[j],
            send_sem=sem,
            recv_sem=recv_sem.at[j, part],
            device_id={"row": row, "col": column},
            device_id_type=pl.DeviceIdType.MESH,
        )

    def arrived(j, part):
        copy(j, part, send_s.at[0, 0, 0], z, sibling).wait_recv()

    def x_copy(r, other, part):
        j = r * n_col + col
        same = other * CORES + k
        to = jnp.where(wanted(j, z, same), same, other * CORES + CORES - 1)
        return copy(j, part, send_x.at[r, other, part], z, to)

    def s_copy(r, cx, part):
        return copy(r * n_col + cx * CORES + k, part, send_s.at[r, cx, part], z, sibling)

    def z_copy(r, up, hop, part):
        to = z + hop if up else z - hop
        return copy(r * n_col + col, part, send_z.at[r, up, hop - 1, part], to, col)

    def to_chips(r, parts, act, keep=lambda other: True):
        j = r * n_col + col
        for dx in range(1, n_x):
            other = (x + dx) % n_x

            @pl.when(chip_wanted(j, z, other) & keep(other))
            def _():
                for part in parts:
                    act(x_copy(r, other, part))

    def to_sibling(r, parts, act):
        @pl.when(wanted(r * n_col + col, z, sibling))
        def _():
            for part in parts:
                act(s_copy(r, x, part))

    def fan_out(r, parts, act):
        to_chips(r, parts, act)
        to_sibling(r, parts, act)

    def onward(r, up, parts, act, hops=None):
        for hop in hops or (UP if up else DOWN):
            to = z + hop if up else z - hop
            gone = (z - r if up else r - z) % REACH

            @pl.when(
                (gone < (2 if up and hop == 1 else 1)) & (to >= 0) & (to < n_row)
                & line_wanted(r * n_col + col, to)
            )
            def _():
                for part in parts:
                    act(z_copy(r, up, hop, part))

    def both_ways(r, parts, act):
        for up in (1, 0):
            @pl.when((r <= z) if up else (r >= z))
            def _():
                onward(r, up, parts, act)

    def start(c):
        c.start()

    def wait_send(c):
        c.wait_send()

    barrier = pltpu.get_barrier_semaphore()

    def signal(sem, row, column):
        pl.semaphore_signal(
            sem, inc=1, device_id={"row": row, "col": column}, device_id_type=pl.DeviceIdType.MESH
        )

    greeted = x * CORES + 1
    for hop in range(1, REACH + 1):
        greeted += jnp.where(z >= hop, 1, 0)

        @pl.when(z + hop < n_row)
        def _():
            signal(barrier, z + hop, col)

        for dx in range(1, n_x) if hop == 1 else ():
            @pl.when(x + dx < n_x)
            def _():
                for c in range(CORES):
                    signal(barrier, z, (x + dx) * CORES + c)

    signal(barrier, z, sibling)
    list_copies = (
        pltpu.make_async_copy(list_ref.at[col, z], lists, list_sem.at[0]),
        pltpu.make_async_copy(count_ref.at[col, pl.ds(z, 1)], counts, list_sem.at[1]),
    )
    own = z * n_col + col
    own_copies = (
        pltpu.make_async_copy(k_ref.at[0], kbuf.at[own], list_sem.at[2]),
        pltpu.make_async_copy(v_ref.at[0], vbuf.at[own], list_sem.at[3]),
    )
    q_copies = [
        pltpu.make_async_copy(
            q_ref.at[0, :, pl.ds(h * head, head)], q_stack.at[pl.ds(h * block, block)], list_sem.at[4 + h]
        )
        for h in range(heads)
    ]
    for c in (*own_copies, *list_copies, *q_copies):
        c.start()

    pl.semaphore_wait(barrier, greeted)

    for hop in UP:
        @pl.when(z >= hop)
        def _():
            signal(ready_z.at[int(hop > 1)], z - hop, col)

    for dx in range(1, n_x):
        @pl.when(x >= dx)
        def _():
            for c in range(CORES):
                signal(ready_x.at[dx - 1], z, (x - dx) * CORES + c)

    for c in own_copies:
        c.wait()

    onward(z, 0, (0, 1), start)
    to_chips(z, (0, 1), start, lambda other: other < x)
    to_sibling(z, (0, 1), start)
    for hop in UP:
        @pl.when(z + hop < n_row)
        def _():
            pl.semaphore_wait(ready_z.at[int(hop > 1)], 1)
            onward(z, 1, (0, 1), start, (hop,))

        if hop == 1:
            for dx in range(1, n_x):
                @pl.when(x + dx < n_x)
                def _():
                    pl.semaphore_wait(ready_x.at[dx - 1], CORES)

            to_chips(z, (0, 1), start, lambda other: other > x)

    acc[...] = jnp.zeros_like(acc)
    run_sum[...] = jnp.zeros_like(run_sum)
    run_max[...] = jnp.full_like(run_max, NEG)
    for c in (*list_copies, *q_copies):
        c.wait()

    def fill(r, carry):
        for p in range(slots):
            hit = jnp.int32(0)
            for s in range(slots):
                hit += jnp.where((lists[r, s] == p) & (s < counts[0, r]), 1, 0)
            bias[r * slots + p] = jnp.where(hit > 0, 0.0, NEG).astype(jnp.float32)
        return carry

    lax.fori_loop(0, n_row, fill, 0)

    def attend(j, count, masked, value_there):
        rows = count * block
        key = kbuf[pl.ds(j, count)].reshape(rows, head)
        s = lax.dot_general(
            key, q_stack[...], (((1,), (1,)), ((), ())), preferred_element_type=jnp.float32
        )
        if masked:
            key_row = lax.broadcasted_iota(jnp.int32, s.shape, 0)
            query_row = lax.broadcasted_iota(jnp.int32, s.shape, 1) % block
            s = jnp.where(key_row - query_row <= (mine - j) * block, s, NEG)
        old = run_max[...]
        parts = [s[b * block : (b + 1) * block] for b in range(count)]
        new = old
        for b in range(count):
            new = jnp.maximum(new, jnp.max(parts[b], axis=0, keepdims=True) + bias[j + b])
        w = jnp.concatenate(
            [jnp.exp2((parts[b] - (new - 3.0 * bias[j + b])) * factor) for b in range(count)], axis=0
        )
        decay = jnp.exp2((old - new) * factor)
        value_there()
        value = vbuf[pl.ds(j, count)].reshape(rows, head)
        run_max[...] = new
        run_sum[...] = run_sum[...] * decay + jnp.sum(w, axis=0, keepdims=True)
        acc[...] = acc[...] * decay + lax.dot_general(
            value, w.astype(jnp.bfloat16), (((0,), (0,)), ((), ())),
            preferred_element_type=jnp.float32,
        )

    def relay_line(r, up):
        j = r * n_col + col

        @pl.when(line_wanted(j, z))
        def _():
            for part in range(2):
                arrived(j, part)
                onward(r, up, (part,), start)
                fan_out(r, (part,), start)

    def relay_chips(r, up):
        for dx in range(1, n_x):
            cx = (x + dx) % n_x
            j = r * n_col + cx * CORES + k

            @pl.when(wanted(j, z, col) & wanted(j, z, sibling))
            def _():
                for part in range(2):
                    arrived(j, part)
                    s_copy(r, cx, part).start()

    def attend_chips(r, dxs):
        for dx in dxs:
            first = r * n_col + ((x + dx) % n_x) * CORES
            theirs = first + 1 - k
            ours = first + k
            alone = wanted(ours, z, col) & jnp.logical_not(wanted(ours, z, sibling))

            def there(part):
                if dx:
                    @pl.when(alone)
                    def _():
                        arrived(ours, part)

                @pl.when(wanted(theirs, z, col))
                def _():
                    arrived(theirs, part)

            there(0)

            @pl.when(first + CORES <= mine)
            def _():
                attend(first, CORES, False, lambda: there(1))

            for c in range(CORES):
                @pl.when(first + c == mine)
                def _():
                    attend(first, c + 1, True, lambda: there(1))

    def at_distance(d, act):
        for r, up in ((z - d, 1), (z + d, 0)):
            @pl.when((r >= 0) & (r < n_row) & ((up > 0) | (d > 0)))
            def _():
                act(r, up)

    def near(t, act):
        d = t + jnp.where(t % REACH == 2, 1, 0) - jnp.where((t % REACH == 0) & (t > 0), 1, 0)
        at_distance(d, act)

    def attend_near(r, up):
        attend_chips(r, (0,))

    def attend_far(r, up):
        attend_chips(r, range(1, n_x))

    at_distance(1, relay_line)
    relay_chips(z, 1)
    near(jnp.int32(2), relay_line)
    attend_near(z, 1)

    def settle():
        both_ways(z, (0, 1), wait_send)
        fan_out(z, (0, 1), wait_send)

        def drain(r, carry):
            @pl.when((r != z) & line_wanted(r * n_col + col, z))
            def _():
                both_ways(r, (0, 1), wait_send)
                fan_out(r, (0, 1), wait_send)

            for dx in range(1, n_x):
                cx = (x + dx) % n_x
                j = r * n_col + cx * CORES + k

                @pl.when(wanted(j, z, sibling) & wanted(j, z, col))
                def _():
                    for part in range(2):
                        s_copy(r, cx, part).wait_send()

            return carry

        lax.fori_loop(0, n_row, drain, 0)

    last = (n_row - 1 + REACH - 1) // REACH * REACH

    def step(t, carry):
        near(t + 3, relay_line)
        near(t + 1, attend_near)
        near(t + 1, relay_chips)
        pl.when(t == last)(settle)
        near(t, attend_far)
        return carry

    lax.fori_loop(0, last + 1, step, 0)

    inverse = 1.0 / run_sum[...]
    for h in range(heads):
        part = slice(h * block, (h + 1) * block)
        o_ref[0, :, h * head : (h + 1) * head] = (acc[:, part] * inverse[:, part]).astype(o_ref.dtype).T


def per_device(n_row, n_col, queries, keys, values, block_list, block_count):
    block, head = keys.shape[1], keys.shape[2]
    wide = queries.shape[1] * (queries.shape[2] // head)
    slots = block_list.shape[3]
    assert queries.shape[1] == block and slots == n_col and block_list.shape[1] == n_row
    blocks = n_row * n_col
    vmem = pl.BlockSpec(memory_space=pltpu.VMEM)
    hbm = pl.BlockSpec(memory_space=pl.ANY)
    return pl.pallas_call(
        functools.partial(kernel, n_row, n_col),
        out_shape=pltpu.VMEM(queries.shape, queries.dtype),
        in_specs=[hbm] * 5,
        out_specs=vmem,
        scratch_shapes=[
            pltpu.VMEM((blocks, block, head), keys.dtype),
            pltpu.VMEM((blocks, block, head), values.dtype),
            pltpu.VMEM((wide, head), queries.dtype),
            pltpu.VMEM((head, wide), jnp.float32),
            pltpu.VMEM((1, wide), jnp.float32),
            pltpu.VMEM((1, wide), jnp.float32),
            pltpu.SMEM((n_row, slots), jnp.int32),
            pltpu.SMEM((1, n_row), jnp.int32),
            pltpu.SMEM((blocks,), jnp.float32),
            pltpu.SemaphoreType.DMA((4 + wide // block,)),
            pltpu.SemaphoreType.DMA((blocks, 2)),
            pltpu.SemaphoreType.REGULAR((len(UP),)),
            pltpu.SemaphoreType.REGULAR((max(1, n_col // CORES - 1),)),
            pltpu.SemaphoreType.DMA((n_row, 2, REACH, 2)),
            pltpu.SemaphoreType.DMA((n_row, n_col // CORES, 2)),
            pltpu.SemaphoreType.DMA((n_row, n_col // CORES, 2)),
        ],
        compiler_params=pltpu.CompilerParams(collective_id=0, has_side_effects=True),
        name="gather_attend",
    )(*(pltpu.with_memory_space_constraint(a, pltpu.HBM) for a in (queries, keys, values, block_list, block_count)))


def solution(mesh):
    placed = (
        P(("groups", "col"), "row", None),
        P(("groups", "row"), "col", None),
        P(("groups", "row"), "col", None),
        P("groups", None, None, None),
        P("groups", None, None),
    )
    return jax.shard_map(
        functools.partial(per_device, mesh.shape["row"], mesh.shape["col"]),
        mesh=mesh,
        in_specs=placed,
        out_specs=P(("groups", "col"), "row", None),
        check_vma=False,
    )
```

```python
import functools

import jax
import jax.numpy as jnp
from jax import lax
from jax.experimental import pallas as pl
from jax.experimental.pallas import tpu as pltpu
from jax.sharding import PartitionSpec as P

NEG = -1e30
LOG2E = 1.4426950408889634
CORES = 2
REACH = 3
UP = (1, REACH)
DOWN = (3, 1, 2)


def kernel(
    n_row, n_col, q_ref, k_ref, v_ref, list_ref, count_ref, o_ref,
    kbuf, vbuf, q_stack, acc, run_max, run_sum, lists, counts, bias,
    list_sem, recv_sem, ready_z, ready_x, send_z, send_x, send_s, send_d,
):
    n_x = n_col // CORES
    block = k_ref.shape[1]
    head = k_ref.shape[2]
    heads = q_ref.shape[2] // head
    slots = lists.shape[1]
    z = lax.axis_index("row")
    col = lax.axis_index("col")
    x = col // CORES
    k = col % CORES
    mine = col * n_row + z
    sibling = x * CORES + (1 - k)
    factor = LOG2E / head**0.5
    cross_first = n_x == 2 and n_row <= REACH + 1

    def wanted(j, at_z, at_col):
        return j <= at_col * n_row + at_z

    def chip_wanted(j, at_z, at_x):
        return j <= (at_x * CORES + CORES - 1) * n_row + at_z

    def line_wanted(j, at_z):
        return j <= (n_col - 1) * n_row + at_z

    def on_line(j, at_z, at_x, r):
        if not cross_first:
            return line_wanted(j, at_z)
        return jnp.where((r == 2) & (at_z == 0), chip_wanted(j, at_z, at_x), line_wanted(j, at_z))

    def copy(j, part, sem, row, column):
        return pltpu.make_async_remote_copy(
            src_ref=(kbuf, vbuf)[part].at[j],
            dst_ref=(kbuf, vbuf)[part].at[j],
            send_sem=sem,
            recv_sem=recv_sem.at[j, part],
            device_id={"row": row, "col": column},
            device_id_type=pl.DeviceIdType.MESH,
        )

    def arrived(j, part):
        copy(j, part, send_s.at[0, 0, 0], z, sibling).wait_recv()

    def x_copy(r, other, part):
        j = r * n_col + col
        same = other * CORES + k
        to = jnp.where(wanted(j, z, same), same, other * CORES + CORES - 1)
        return copy(j, part, send_x.at[r, other, part], z, to)

    def s_copy(r, cx, part):
        return copy(r * n_col + cx * CORES + k, part, send_s.at[r, cx, part], z, sibling)

    def z_copy(r, up, hop, part):
        to = z + hop if up else z - hop
        return copy(r * n_col + col, part, send_z.at[r, up, hop - 1, part], to, col)

    def to_chips(r, parts, act, keep=lambda other: True):
        j = r * n_col + col
        for dx in range(1, n_x):
            other = (x + dx) % n_x

            @pl.when(chip_wanted(j, z, other) & keep(other))
            def _():
                for part in parts:
                    act(x_copy(r, other, part))

    def to_sibling(r, parts, act):
        @pl.when(wanted(r * n_col + col, z, sibling))
        def _():
            for part in parts:
                act(s_copy(r, x, part))

    def fan_out(r, parts, act):
        to_chips(r, parts, act)
        to_sibling(r, parts, act)

    def onward(r, up, parts, act, hops=None):
        for hop in hops or (UP if up else DOWN):
            to = z + hop if up else z - hop
            gone = (z - r if up else r - z) % REACH

            @pl.when(
                (gone < (2 if up and hop == 1 else 1)) & (to >= 0) & (to < n_row)
                & on_line(r * n_col + col, to, x, r)
            )
            def _():
                for part in parts:
                    act(z_copy(r, up, hop, part))

    def both_ways(r, parts, act):
        for up in (1, 0):
            @pl.when((r <= z) if up else (r >= z))
            def _():
                onward(r, up, parts, act)

    def start(c):
        c.start()

    def wait_send(c):
        c.wait_send()

    barrier = pltpu.get_barrier_semaphore()

    def signal(sem, row, column):
        pl.semaphore_signal(
            sem, inc=1, device_id={"row": row, "col": column}, device_id_type=pl.DeviceIdType.MESH
        )

    greeted = x * CORES + 1
    for hop in range(1, REACH + 1):
        greeted += jnp.where(z >= hop, 1, 0)

        @pl.when(z + hop < n_row)
        def _():
            signal(barrier, z + hop, col)

        for dx in range(1, n_x) if hop == 1 else ():
            @pl.when(x + dx < n_x)
            def _():
                for c in range(CORES):
                    signal(barrier, z, (x + dx) * CORES + c)

    signal(barrier, z, sibling)
    list_copies = (
        pltpu.make_async_copy(list_ref.at[col, z], lists, list_sem.at[0]),
        pltpu.make_async_copy(count_ref.at[col, pl.ds(z, 1)], counts, list_sem.at[1]),
    )
    own = z * n_col + col
    own_copies = (
        pltpu.make_async_copy(k_ref.at[0], kbuf.at[own], list_sem.at[2]),
        pltpu.make_async_copy(v_ref.at[0], vbuf.at[own], list_sem.at[3]),
    )
    q_copies = [
        pltpu.make_async_copy(
            q_ref.at[0, :, pl.ds(h * head, head)], q_stack.at[pl.ds(h * block, block)], list_sem.at[4 + h]
        )
        for h in range(heads)
    ]
    for c in (*own_copies, *list_copies, *q_copies):
        c.start()

    pl.semaphore_wait(barrier, greeted)

    for hop in UP:
        @pl.when(z >= hop)
        def _():
            signal(ready_z.at[int(hop > 1)], z - hop, col)

    for dx in range(1, n_x):
        @pl.when(x >= dx)
        def _():
            for c in range(CORES):
                signal(ready_x.at[dx - 1], z, (x - dx) * CORES + c)

    for c in own_copies:
        c.wait()

    onward(z, 0, (0, 1), start)
    to_chips(z, (0, 1), start, lambda other: other < x)
    to_sibling(z, (0, 1), start)
    for hop in UP:
        @pl.when(z + hop < n_row)
        def _():
            pl.semaphore_wait(ready_z.at[int(hop > 1)], 1)
            onward(z, 1, (0, 1), start, (hop,))

        if hop == 1:
            for dx in range(1, n_x):
                @pl.when(x + dx < n_x)
                def _():
                    pl.semaphore_wait(ready_x.at[dx - 1], CORES)

            to_chips(z, (0, 1), start, lambda other: other > x)

    acc[...] = jnp.zeros_like(acc)
    run_sum[...] = jnp.zeros_like(run_sum)
    run_max[...] = jnp.full_like(run_max, NEG)
    for c in (*list_copies, *q_copies):
        c.wait()

    def fill(r, carry):
        for p in range(slots):
            hit = jnp.int32(0)
            for s in range(slots):
                hit += jnp.where((lists[r, s] == p) & (s < counts[0, r]), 1, 0)
            bias[r * slots + p] = jnp.where(hit > 0, 0.0, NEG).astype(jnp.float32)
        return carry

    lax.fori_loop(0, n_row, fill, 0)

    def attend(j, count, masked, value_there):
        rows = count * block
        key = kbuf[pl.ds(j, count)].reshape(rows, head)
        s = lax.dot_general(
            key, q_stack[...], (((1,), (1,)), ((), ())), preferred_element_type=jnp.float32
        )
        if masked:
            key_row = lax.broadcasted_iota(jnp.int32, s.shape, 0)
            query_row = lax.broadcasted_iota(jnp.int32, s.shape, 1) % block
            s = jnp.where(key_row - query_row <= (mine - j) * block, s, NEG)
        old = run_max[...]
        parts = [s[b * block : (b + 1) * block] for b in range(count)]
        new = old
        for b in range(count):
            new = jnp.maximum(new, jnp.max(parts[b], axis=0, keepdims=True) + bias[j + b])
        w = jnp.concatenate(
            [jnp.exp2((parts[b] - (new - 3.0 * bias[j + b])) * factor) for b in range(count)], axis=0
        )
        decay = jnp.exp2((old - new) * factor)
        value_there()
        value = vbuf[pl.ds(j, count)].reshape(rows, head)
        run_max[...] = new
        run_sum[...] = run_sum[...] * decay + jnp.sum(w, axis=0, keepdims=True)
        acc[...] = acc[...] * decay + lax.dot_general(
            value, w.astype(jnp.bfloat16), (((0,), (0,)), ((), ())),
            preferred_element_type=jnp.float32,
        )

    def relay_line(r, up):
        j = r * n_col + col

        @pl.when(on_line(j, z, x, r))
        def _():
            for part in range(2):
                arrived(j, part)
                onward(r, up, (part,), start)
                fan_out(r, (part,), start)

    def passed_down(j):
        return (z == 2) & chip_wanted(j, 0, x) & jnp.logical_not(chip_wanted(j, 0, 1 - x))

    def own_receiver(j, kc):
        if kc == 0:
            return jnp.where(wanted(j, z, x * CORES), 0, 1) == k
        return k == 1

    def cross_own(act_wait, act_send, act_sibling):
        for kc in range(CORES):
            j = z * n_col + (1 - x) * CORES + kc

            @pl.when((x > 0) & passed_down(j) & own_receiver(j, kc))
            def _():
                for part in range(2):
                    act_wait(j, part)
                    act_send(copy(j, part, send_d.at[kc, part], 0, col))

                    if act_sibling is not None:
                        @pl.when((k == kc) & wanted(j, z, sibling))
                        def _():
                            act_sibling(s_copy(z, 1 - x, part))

    def relay_own():
        if cross_first:
            cross_own(arrived, start, start)
        relay_chips(z, 1)

    def relay_chips(r, up):
        for dx in range(1, n_x):
            cx = (x + dx) % n_x
            j = r * n_col + cx * CORES + k

            later = jnp.logical_not((r == z) & (x > 0) & passed_down(j)) if cross_first else True

            @pl.when(wanted(j, z, col) & wanted(j, z, sibling) & later)
            def _():
                for part in range(2):
                    arrived(j, part)
                    s_copy(r, cx, part).start()

    def attend_chips(r, dxs):
        for dx in dxs:
            first = r * n_col + ((x + dx) % n_x) * CORES
            theirs = first + 1 - k
            ours = first + k
            alone = wanted(ours, z, col) & jnp.logical_not(wanted(ours, z, sibling))
            sent = wanted(theirs, z, col)
            if cross_first and dx:
                early = (r == z) & (x > 0)
                alone &= jnp.logical_not(early & passed_down(ours))
                sent &= jnp.logical_not(early & passed_down(theirs) & jnp.logical_not(wanted(theirs, z, sibling)))

            def there(part):
                if dx:
                    @pl.when(alone)
                    def _():
                        arrived(ours, part)

                @pl.when(sent)
                def _():
                    arrived(theirs, part)

            there(0)

            @pl.when(first + CORES <= mine)
            def _():
                attend(first, CORES, False, lambda: there(1))

            for c in range(CORES):
                @pl.when(first + c == mine)
                def _():
                    attend(first, c + 1, True, lambda: there(1))

    def at_distance(d, act):
        for r, up in ((z - d, 1), (z + d, 0)):
            @pl.when((r >= 0) & (r < n_row) & ((up > 0) | (d > 0)))
            def _():
                act(r, up)

    def near(t, act, swap=True):
        d = t + jnp.where(t % REACH == 2, 1, 0) - jnp.where((t % REACH == 0) & (t > 0), 1, 0)
        at_distance(jnp.where(swap, d, t), act)

    def attend_near(r, up):
        attend_chips(r, (0,))

    def attend_far(r, up):
        attend_chips(r, range(1, n_x))

    attend_near(z, 1)
    at_distance(1, relay_line)
    relay_own()
    near(jnp.int32(2), relay_line)

    def settle_lines():
        both_ways(z, (0, 1), wait_send)
        fan_out(z, (0, 1), wait_send)

        def drain(r, carry):
            @pl.when((r != z) & on_line(r * n_col + col, z, x, r))
            def _():
                both_ways(r, (0, 1), wait_send)
                fan_out(r, (0, 1), wait_send)

            return carry

        lax.fori_loop(0, n_row, drain, 0)

    def settle_chips():
        if cross_first:
            cross_own(lambda j, part: None, wait_send, None)

        def drain(r, carry):
            for dx in range(1, n_x):
                cx = (x + dx) % n_x
                j = r * n_col + cx * CORES + k

                @pl.when(wanted(j, z, sibling) & wanted(j, z, col))
                def _():
                    for part in range(2):
                        s_copy(r, cx, part).wait_send()

            return carry

        lax.fori_loop(0, n_row, drain, 0)

    last = (n_row - 1 + REACH - 1) // REACH * REACH

    paired = (x > 0) | (z < REACH)

    def step(t, carry):
        near(t + 1, attend_near)
        near(t + 3, relay_line)
        near(t + 1, relay_chips)
        pl.when(t == last - 1)(settle_lines)
        pl.when(t == last - jnp.where(paired, 0, 1))(settle_chips)
        near(t, attend_far, paired)
        return carry

    lax.fori_loop(0, last + 1, step, 0)

    inverse = 1.0 / run_sum[...]
    for h in range(heads):
        part = slice(h * block, (h + 1) * block)
        o_ref[0, :, h * head : (h + 1) * head] = (acc[:, part] * inverse[:, part]).astype(o_ref.dtype).T


def per_device(n_row, n_col, queries, keys, values, block_list, block_count):
    block, head = keys.shape[1], keys.shape[2]
    wide = queries.shape[1] * (queries.shape[2] // head)
    slots = block_list.shape[3]
    assert queries.shape[1] == block and slots == n_col and block_list.shape[1] == n_row
    blocks = n_row * n_col
    vmem = pl.BlockSpec(memory_space=pltpu.VMEM)
    hbm = pl.BlockSpec(memory_space=pl.ANY)
    return pl.pallas_call(
        functools.partial(kernel, n_row, n_col),
        out_shape=pltpu.VMEM(queries.shape, queries.dtype),
        in_specs=[hbm] * 5,
        out_specs=vmem,
        scratch_shapes=[
            pltpu.VMEM((blocks, block, head), keys.dtype),
            pltpu.VMEM((blocks, block, head), values.dtype),
            pltpu.VMEM((wide, head), queries.dtype),
            pltpu.VMEM((head, wide), jnp.float32),
            pltpu.VMEM((1, wide), jnp.float32),
            pltpu.VMEM((1, wide), jnp.float32),
            pltpu.SMEM((n_row, slots), jnp.int32),
            pltpu.SMEM((1, n_row), jnp.int32),
            pltpu.SMEM((blocks,), jnp.float32),
            pltpu.SemaphoreType.DMA((4 + wide // block,)),
            pltpu.SemaphoreType.DMA((blocks, 2)),
            pltpu.SemaphoreType.REGULAR((len(UP),)),
            pltpu.SemaphoreType.REGULAR((max(1, n_col // CORES - 1),)),
            pltpu.SemaphoreType.DMA((n_row, 2, REACH, 2)),
            pltpu.SemaphoreType.DMA((n_row, n_col // CORES, 2)),
            pltpu.SemaphoreType.DMA((n_row, n_col // CORES, 2)),
            pltpu.SemaphoreType.DMA((CORES, 2)),
        ],
        compiler_params=pltpu.CompilerParams(collective_id=0, has_side_effects=True),
        name="gather_attend",
    )(*(pltpu.with_memory_space_constraint(a, pltpu.HBM) for a in (queries, keys, values, block_list, block_count)))


def solution(mesh):
    placed = (
        P(("groups", "col"), "row", None),
        P(("groups", "row"), "col", None),
        P(("groups", "row"), "col", None),
        P("groups", None, None, None),
        P("groups", None, None),
    )
    return jax.shard_map(
        functools.partial(per_device, mesh.shape["row"], mesh.shape["col"]),
        mesh=mesh,
        in_specs=placed,
        out_specs=P(("groups", "col"), "row", None),
        check_vma=False,
    )
```

```python
import functools

import jax
import jax.numpy as jnp
from jax import lax
from jax.experimental import pallas as pl
from jax.experimental.pallas import tpu as pltpu
from jax.sharding import PartitionSpec as P

NEG = -1e30
LOG2E = 1.4426950408889634
CORES = 2
REACH = 3
UP = (1, REACH)
DOWN = (3, 1, 2)


def kernel(
    n_row, n_col, q_ref, k_ref, v_ref, list_ref, count_ref, o_ref,
    kbuf, vbuf, q_stack, acc, run_max, run_sum, lists, counts, bias,
    list_sem, recv_sem, ready_z, ready_x, ready_d, send_z, send_x, send_s, send_d, send_e,
):
    n_x = n_col // CORES
    block = k_ref.shape[1]
    head = k_ref.shape[2]
    heads = q_ref.shape[2] // head
    slots = lists.shape[1]
    z = lax.axis_index("row")
    col = lax.axis_index("col")
    x = col // CORES
    k = col % CORES
    mine = col * n_row + z
    sibling = x * CORES + (1 - k)
    factor = LOG2E / head**0.5
    cross_first = n_x == 2 and n_row <= REACH + 1

    def wanted(j, at_z, at_col):
        return j <= at_col * n_row + at_z

    def chip_wanted(j, at_z, at_x):
        return j <= (at_x * CORES + CORES - 1) * n_row + at_z

    def line_wanted(j, at_z):
        return j <= (n_col - 1) * n_row + at_z

    def on_line(j, at_z, at_x, r):
        if not cross_first:
            return line_wanted(j, at_z)
        return jnp.where((r == 2) & (at_z == 0), chip_wanted(j, at_z, at_x), line_wanted(j, at_z))

    def copy(j, part, sem, row, column):
        return pltpu.make_async_remote_copy(
            src_ref=(kbuf, vbuf)[part].at[j],
            dst_ref=(kbuf, vbuf)[part].at[j],
            send_sem=sem,
            recv_sem=recv_sem.at[j, part],
            device_id={"row": row, "col": column},
            device_id_type=pl.DeviceIdType.MESH,
        )

    def arrived(j, part):
        copy(j, part, send_s.at[0, 0, 0], z, sibling).wait_recv()

    def x_copy(r, other, part):
        j = r * n_col + col
        same = other * CORES + k
        to = jnp.where(wanted(j, z, same), same, other * CORES + CORES - 1)
        return copy(j, part, send_x.at[r, other, part], z, to)

    def s_copy(r, cx, part):
        return copy(r * n_col + cx * CORES + k, part, send_s.at[r, cx, part], z, sibling)

    def z_copy(r, up, hop, part):
        to = z + hop if up else z - hop
        return copy(r * n_col + col, part, send_z.at[r, up, hop - 1, part], to, col)

    def to_chips(r, parts, act, keep=lambda other: True):
        j = r * n_col + col
        for dx in range(1, n_x):
            other = (x + dx) % n_x

            ahead = (r == 0) & (z == 2) & (x > 0) if cross_first else False

            @pl.when(chip_wanted(j, z, other) & keep(other) & jnp.logical_not(ahead))
            def _():
                for part in parts:
                    act(x_copy(r, other, part))

    def to_sibling(r, parts, act):
        @pl.when(wanted(r * n_col + col, z, sibling))
        def _():
            for part in parts:
                act(s_copy(r, x, part))

    def fan_out(r, parts, act):
        to_chips(r, parts, act)
        to_sibling(r, parts, act)

    def onward(r, up, parts, act, hops=None):
        for hop in hops or (UP if up else DOWN):
            to = z + hop if up else z - hop
            gone = (z - r if up else r - z) % REACH

            @pl.when(
                (gone < (2 if up and hop == 1 else 1)) & (to >= 0) & (to < n_row)
                & on_line(r * n_col + col, to, x, r)
            )
            def _():
                for part in parts:
                    act(z_copy(r, up, hop, part))

    def both_ways(r, parts, act):
        for up in (1, 0):
            @pl.when((r <= z) if up else (r >= z))
            def _():
                onward(r, up, parts, act)

    def start(c):
        c.start()

    def wait_send(c):
        c.wait_send()

    barrier = pltpu.get_barrier_semaphore()

    def signal(sem, row, column):
        pl.semaphore_signal(
            sem, inc=1, device_id={"row": row, "col": column}, device_id_type=pl.DeviceIdType.MESH
        )

    greeted = x * CORES + 1
    for hop in range(1, REACH + 1):
        greeted += jnp.where(z >= hop, 1, 0)

        @pl.when(z + hop < n_row)
        def _():
            signal(barrier, z + hop, col)

        for dx in range(1, n_x) if hop == 1 else ():
            @pl.when(x + dx < n_x)
            def _():
                for c in range(CORES):
                    signal(barrier, z, (x + dx) * CORES + c)

    signal(barrier, z, sibling)
    list_copies = (
        pltpu.make_async_copy(list_ref.at[col, z], lists, list_sem.at[0]),
        pltpu.make_async_copy(count_ref.at[col, pl.ds(z, 1)], counts, list_sem.at[1]),
    )
    own = z * n_col + col
    own_copies = (
        pltpu.make_async_copy(k_ref.at[0], kbuf.at[own], list_sem.at[2]),
        pltpu.make_async_copy(v_ref.at[0], vbuf.at[own], list_sem.at[3]),
    )
    q_copies = [
        pltpu.make_async_copy(
            q_ref.at[0, :, pl.ds(h * head, head)], q_stack.at[pl.ds(h * block, block)], list_sem.at[4 + h]
        )
        for h in range(heads)
    ]
    for c in (*own_copies, *list_copies, *q_copies):
        c.start()

    pl.semaphore_wait(barrier, greeted)

    for hop in UP:
        @pl.when(z >= hop)
        def _():
            signal(ready_z.at[int(hop > 1)], z - hop, col)

    for dx in range(1, n_x):
        @pl.when(x >= dx)
        def _():
            for c in range(CORES):
                signal(ready_x.at[dx - 1], z, (x - dx) * CORES + c)

    for c in own_copies:
        c.wait()

    onward(z, 0, (0, 1), start)
    to_chips(z, (0, 1), start, lambda other: other < x)
    to_sibling(z, (0, 1), start)
    for hop in UP:
        @pl.when(z + hop < n_row)
        def _():
            pl.semaphore_wait(ready_z.at[int(hop > 1)], 1)
            onward(z, 1, (0, 1), start, (hop,))

        if hop == 1:
            for dx in range(1, n_x):
                @pl.when(x + dx < n_x)
                def _():
                    pl.semaphore_wait(ready_x.at[dx - 1], CORES)

            to_chips(z, (0, 1), start, lambda other: other > x)
            if cross_first:
                @pl.when((z == 1) & (z + 1 < n_row))
                def _():
                    @pl.when(x == 0)
                    def _():
                        for c in range(CORES):
                            signal(ready_d, z, CORES + c)

                    @pl.when(x > 0)
                    def _():
                        pl.semaphore_wait(ready_d, CORES)

    acc[...] = jnp.zeros_like(acc)
    run_sum[...] = jnp.zeros_like(run_sum)
    run_max[...] = jnp.full_like(run_max, NEG)
    for c in (*list_copies, *q_copies):
        c.wait()

    def fill(r, carry):
        for p in range(slots):
            hit = jnp.int32(0)
            for s in range(slots):
                hit += jnp.where((lists[r, s] == p) & (s < counts[0, r]), 1, 0)
            bias[r * slots + p] = jnp.where(hit > 0, 0.0, NEG).astype(jnp.float32)
        return carry

    lax.fori_loop(0, n_row, fill, 0)

    def attend(j, count, masked, value_there):
        rows = count * block
        key = kbuf[pl.ds(j, count)].reshape(rows, head)
        s = lax.dot_general(
            key, q_stack[...], (((1,), (1,)), ((), ())), preferred_element_type=jnp.float32
        )
        if masked:
            key_row = lax.broadcasted_iota(jnp.int32, s.shape, 0)
            query_row = lax.broadcasted_iota(jnp.int32, s.shape, 1) % block
            s = jnp.where(key_row - query_row <= (mine - j) * block, s, NEG)
        old = run_max[...]
        parts = [s[b * block : (b + 1) * block] for b in range(count)]
        new = old
        for b in range(count):
            new = jnp.maximum(new, jnp.max(parts[b], axis=0, keepdims=True) + bias[j + b])
        w = jnp.concatenate(
            [jnp.exp2((parts[b] - (new - 3.0 * bias[j + b])) * factor) for b in range(count)], axis=0
        )
        decay = jnp.exp2((old - new) * factor)
        value_there()
        value = vbuf[pl.ds(j, count)].reshape(rows, head)
        run_max[...] = new
        run_sum[...] = run_sum[...] * decay + jnp.sum(w, axis=0, keepdims=True)
        acc[...] = acc[...] * decay + lax.dot_general(
            value, w.astype(jnp.bfloat16), (((0,), (0,)), ((), ())),
            preferred_element_type=jnp.float32,
        )

    def ahead_copies(r, part, act):
        j = r * n_col + col

        @pl.when((r == 0) & (z == 1) & (z + 1 < n_row) & (x > 0) & chip_wanted(j, z + 1, 0))
        def _():
            to = jnp.where(wanted(j, z + 1, k), k, CORES - 1)
            act(copy(j, part, send_e.at[part], z + 1, to))

    def relay_line(r, up):
        j = r * n_col + col

        @pl.when(on_line(j, z, x, r))
        def _():
            for part in range(2):
                arrived(j, part)
                onward(r, up, (part,), start)
                fan_out(r, (part,), start)

            if cross_first and up:
                for part in range(2):
                    ahead_copies(r, part, start)

    def passed_down(j):
        return (z == 2) & chip_wanted(j, 0, x) & jnp.logical_not(chip_wanted(j, 0, 1 - x))

    def own_receiver(j, kc):
        if kc == 0:
            return jnp.where(wanted(j, z, x * CORES), 0, 1) == k
        return k == 1

    def cross_own(act_wait, act_send, act_sibling):
        for kc in range(CORES):
            j = z * n_col + (1 - x) * CORES + kc

            @pl.when((x > 0) & passed_down(j) & own_receiver(j, kc))
            def _():
                for part in range(2):
                    act_wait(j, part)
                    act_send(copy(j, part, send_d.at[kc, part], 0, col))

                    if act_sibling is not None:
                        @pl.when((k == kc) & wanted(j, z, sibling))
                        def _():
                            act_sibling(s_copy(z, 1 - x, part))

    def relay_own():
        if cross_first:
            cross_own(arrived, start, start)
        relay_chips(z, 1)

    def relay_chips(r, up):
        for dx in range(1, n_x):
            cx = (x + dx) % n_x
            j = r * n_col + cx * CORES + k

            later = jnp.logical_not((r == z) & (x > 0) & passed_down(j)) if cross_first else True

            @pl.when(wanted(j, z, col) & wanted(j, z, sibling) & later)
            def _():
                for part in range(2):
                    arrived(j, part)
                    s_copy(r, cx, part).start()

    def attend_chips(r, dxs):
        for dx in dxs:
            first = r * n_col + ((x + dx) % n_x) * CORES
            theirs = first + 1 - k
            ours = first + k
            alone = wanted(ours, z, col) & jnp.logical_not(wanted(ours, z, sibling))
            sent = wanted(theirs, z, col)
            if cross_first and dx:
                early = (r == z) & (x > 0)
                alone &= jnp.logical_not(early & passed_down(ours))
                sent &= jnp.logical_not(early & passed_down(theirs) & jnp.logical_not(wanted(theirs, z, sibling)))

            def there(part):
                if dx:
                    @pl.when(alone)
                    def _():
                        arrived(ours, part)

                @pl.when(sent)
                def _():
                    arrived(theirs, part)

            there(0)

            @pl.when(first + CORES <= mine)
            def _():
                attend(first, CORES, False, lambda: there(1))

            for c in range(CORES):
                @pl.when(first + c == mine)
                def _():
                    attend(first, c + 1, True, lambda: there(1))

    def at_distance(d, act):
        for r, up in ((z - d, 1), (z + d, 0)):
            @pl.when((r >= 0) & (r < n_row) & ((up > 0) | (d > 0)))
            def _():
                act(r, up)

    def near(t, act, swap=True):
        d = t + jnp.where(t % REACH == 2, 1, 0) - jnp.where((t % REACH == 0) & (t > 0), 1, 0)
        at_distance(jnp.where(swap, d, t), act)

    def attend_near(r, up):
        attend_chips(r, (0,))

    def attend_far(r, up):
        attend_chips(r, range(1, n_x))

    attend_near(z, 1)
    at_distance(1, relay_line)
    relay_own()
    near(jnp.int32(2), relay_line)

    def settle_lines():
        if cross_first:
            for part in range(2):
                ahead_copies(0, part, wait_send)

        both_ways(z, (0, 1), wait_send)
        fan_out(z, (0, 1), wait_send)

        def drain(r, carry):
            @pl.when((r != z) & on_line(r * n_col + col, z, x, r))
            def _():
                both_ways(r, (0, 1), wait_send)
                fan_out(r, (0, 1), wait_send)

            return carry

        lax.fori_loop(0, n_row, drain, 0)

    def settle_chips():
        if cross_first:
            cross_own(lambda j, part: None, wait_send, None)

        def drain(r, carry):
            for dx in range(1, n_x):
                cx = (x + dx) % n_x
                j = r * n_col + cx * CORES + k

                @pl.when(wanted(j, z, sibling) & wanted(j, z, col))
                def _():
                    for part in range(2):
                        s_copy(r, cx, part).wait_send()

            return carry

        lax.fori_loop(0, n_row, drain, 0)

    last = (n_row - 1 + REACH - 1) // REACH * REACH

    paired = (x > 0) | (z < REACH)

    def step(t, carry):
        near(t + 1, attend_near)
        near(t + 3, relay_line)
        pl.when(t == last - 2)(settle_lines)
        near(t + 1, relay_chips)
        near(t, attend_far, paired)
        return carry

    lax.fori_loop(0, last + 1, step, 0)
    settle_chips()

    inverse = 1.0 / run_sum[...]
    for h in range(heads):
        part = slice(h * block, (h + 1) * block)
        o_ref[0, :, h * head : (h + 1) * head] = (acc[:, part] * inverse[:, part]).astype(o_ref.dtype).T


def per_device(n_row, n_col, queries, keys, values, block_list, block_count):
    block, head = keys.shape[1], keys.shape[2]
    wide = queries.shape[1] * (queries.shape[2] // head)
    slots = block_list.shape[3]
    assert queries.shape[1] == block and slots == n_col and block_list.shape[1] == n_row
    blocks = n_row * n_col
    vmem = pl.BlockSpec(memory_space=pltpu.VMEM)
    hbm = pl.BlockSpec(memory_space=pl.ANY)
    return pl.pallas_call(
        functools.partial(kernel, n_row, n_col),
        out_shape=pltpu.VMEM(queries.shape, queries.dtype),
        in_specs=[hbm] * 5,
        out_specs=vmem,
        scratch_shapes=[
            pltpu.VMEM((blocks, block, head), keys.dtype),
            pltpu.VMEM((blocks, block, head), values.dtype),
            pltpu.VMEM((wide, head), queries.dtype),
            pltpu.VMEM((head, wide), jnp.float32),
            pltpu.VMEM((1, wide), jnp.float32),
            pltpu.VMEM((1, wide), jnp.float32),
            pltpu.SMEM((n_row, slots), jnp.int32),
            pltpu.SMEM((1, n_row), jnp.int32),
            pltpu.SMEM((blocks,), jnp.float32),
            pltpu.SemaphoreType.DMA((4 + wide // block,)),
            pltpu.SemaphoreType.DMA((blocks, 2)),
            pltpu.SemaphoreType.REGULAR((len(UP),)),
            pltpu.SemaphoreType.REGULAR((max(1, n_col // CORES - 1),)),
            pltpu.SemaphoreType.REGULAR,
            pltpu.SemaphoreType.DMA((n_row, 2, REACH, 2)),
            pltpu.SemaphoreType.DMA((n_row, n_col // CORES, 2)),
            pltpu.SemaphoreType.DMA((n_row, n_col // CORES, 2)),
            pltpu.SemaphoreType.DMA((CORES, 2)),
            pltpu.SemaphoreType.DMA((2,)),
        ],
        compiler_params=pltpu.CompilerParams(collective_id=0, has_side_effects=True),
        name="gather_attend",
    )(*(pltpu.with_memory_space_constraint(a, pltpu.HBM) for a in (queries, keys, values, block_list, block_count)))


def solution(mesh):
    placed = (
        P(("groups", "col"), "row", None),
        P(("groups", "row"), "col", None),
        P(("groups", "row"), "col", None),
        P("groups", None, None, None),
        P("groups", None, None),
    )
    return jax.shard_map(
        functools.partial(per_device, mesh.shape["row"], mesh.shape["col"]),
        mesh=mesh,
        in_specs=placed,
        out_specs=P(("groups", "col"), "row", None),
        check_vma=False,
    )
```

```python
import functools

import jax
import jax.numpy as jnp
from jax import lax
from jax.experimental import pallas as pl
from jax.experimental.pallas import tpu as pltpu
from jax.sharding import PartitionSpec as P

NEG = -1e30
LOG2E = 1.4426950408889634
CORES = 2
REACH = 3
UP = (1, REACH)
DOWN = (3, 1, 2)


def kernel(
    n_row, n_col, q_ref, k_ref, v_ref, list_ref, count_ref, o_ref,
    kbuf, vbuf, q_stack, acc, run_max, run_sum, lists, counts, bias,
    list_sem, recv_sem, ready_z, ready_x, ready_d, send_z, send_x, send_s, send_d, send_e,
):
    n_x = n_col // CORES
    block = k_ref.shape[1]
    head = k_ref.shape[2]
    heads = q_ref.shape[2] // head
    slots = lists.shape[1]
    z = lax.axis_index("row")
    col = lax.axis_index("col")
    x = col // CORES
    k = col % CORES
    mine = col * n_row + z
    sibling = x * CORES + (1 - k)
    factor = LOG2E / head**0.5
    short = n_row <= REACH + 1
    cross_first = n_x == 2 and short

    def wanted(j, at_z, at_col):
        return j <= at_col * n_row + at_z

    def chip_wanted(j, at_z, at_x):
        return j <= (at_x * CORES + CORES - 1) * n_row + at_z

    def line_wanted(j, at_z):
        return j <= (n_col - 1) * n_row + at_z

    def on_line(j, at_z, at_x, r):
        if not cross_first:
            return line_wanted(j, at_z)
        return jnp.where((r == 2) & (at_z == 0), chip_wanted(j, at_z, at_x), line_wanted(j, at_z))

    def copy(j, part, sem, row, column):
        return pltpu.make_async_remote_copy(
            src_ref=(kbuf, vbuf)[part].at[j],
            dst_ref=(kbuf, vbuf)[part].at[j],
            send_sem=sem,
            recv_sem=recv_sem.at[j, part],
            device_id={"row": row, "col": column},
            device_id_type=pl.DeviceIdType.MESH,
        )

    def arrived(j, part):
        copy(j, part, send_s.at[0, 0, 0], z, sibling).wait_recv()

    def x_copy(r, other, part):
        j = r * n_col + col
        same = other * CORES + k
        to = jnp.where(wanted(j, z, same), same, other * CORES + CORES - 1)
        return copy(j, part, send_x.at[r, other, part], z, to)

    def s_copy(r, cx, part):
        return copy(r * n_col + cx * CORES + k, part, send_s.at[r, cx, part], z, sibling)

    def z_copy(r, up, hop, part):
        to = z + hop if up else z - hop
        return copy(r * n_col + col, part, send_z.at[r, up, hop - 1, part], to, col)

    def to_chips(r, parts, act, keep=lambda other: True):
        j = r * n_col + col
        for dx in range(1, n_x):
            other = (x + dx) % n_x

            ahead = (r == 0) & (z == 2) & (x > 0) if cross_first else False

            @pl.when(chip_wanted(j, z, other) & keep(other) & jnp.logical_not(ahead))
            def _():
                for part in parts:
                    act(x_copy(r, other, part))

    def to_sibling(r, parts, act):
        @pl.when(wanted(r * n_col + col, z, sibling))
        def _():
            for part in parts:
                act(s_copy(r, x, part))

    def fan_out(r, parts, act):
        to_chips(r, parts, act)
        to_sibling(r, parts, act)

    def onward(r, up, parts, act, hops=None):
        for hop in hops or (UP if up else DOWN):
            to = z + hop if up else z - hop
            gone = (z - r if up else r - z) % REACH

            @pl.when(
                (gone < (2 if up and hop == 1 else 1)) & (to >= 0) & (to < n_row)
                & on_line(r * n_col + col, to, x, r)
            )
            def _():
                for part in parts:
                    act(z_copy(r, up, hop, part))

    def both_ways(r, parts, act):
        for up in (1, 0):
            @pl.when((r <= z) if up else (r >= z))
            def _():
                onward(r, up, parts, act)

    def start(c):
        c.start()

    def wait_send(c):
        c.wait_send()

    barrier = pltpu.get_barrier_semaphore()

    def signal(sem, row, column):
        pl.semaphore_signal(
            sem, inc=1, device_id={"row": row, "col": column}, device_id_type=pl.DeviceIdType.MESH
        )

    greeted = x * CORES + 1
    for hop in range(1, REACH + 1):
        greeted += jnp.where(z >= hop, 1, 0)

        @pl.when(z + hop < n_row)
        def _():
            signal(barrier, z + hop, col)

        for dx in range(1, n_x) if hop == 1 else ():
            @pl.when(x + dx < n_x)
            def _():
                for c in range(CORES):
                    signal(barrier, z, (x + dx) * CORES + c)

    signal(barrier, z, sibling)
    list_copies = (
        pltpu.make_async_copy(list_ref.at[col, z], lists, list_sem.at[0]),
        pltpu.make_async_copy(count_ref.at[col, pl.ds(z, 1)], counts, list_sem.at[1]),
    )
    own = z * n_col + col
    own_copies = (
        pltpu.make_async_copy(k_ref.at[0], kbuf.at[own], list_sem.at[2]),
        pltpu.make_async_copy(v_ref.at[0], vbuf.at[own], list_sem.at[3]),
    )
    q_copies = [
        pltpu.make_async_copy(
            q_ref.at[0, :, pl.ds(h * head, head)], q_stack.at[pl.ds(h * block, block)], list_sem.at[4 + h]
        )
        for h in range(heads)
    ]
    for c in (*own_copies, *list_copies, *q_copies):
        c.start()

    pl.semaphore_wait(barrier, greeted)

    for hop in UP:
        @pl.when(z >= hop)
        def _():
            signal(ready_z.at[int(hop > 1)], z - hop, col)

    for dx in range(1, n_x):
        @pl.when(x >= dx)
        def _():
            for c in range(CORES):
                signal(ready_x.at[dx - 1], z, (x - dx) * CORES + c)

    for c in own_copies:
        c.wait()

    onward(z, 0, (0, 1), start)
    to_chips(z, (0, 1), start, lambda other: other < x)
    to_sibling(z, (0, 1), start)
    for hop in UP:
        @pl.when(z + hop < n_row)
        def _():
            pl.semaphore_wait(ready_z.at[int(hop > 1)], 1)
            onward(z, 1, (0, 1), start, (hop,))

        if hop == 1:
            for dx in range(1, n_x):
                @pl.when(x + dx < n_x)
                def _():
                    pl.semaphore_wait(ready_x.at[dx - 1], CORES)

            to_chips(z, (0, 1), start, lambda other: other > x)
            if cross_first:
                @pl.when((z == 1) & (z + 1 < n_row))
                def _():
                    @pl.when(x == 0)
                    def _():
                        for c in range(CORES):
                            signal(ready_d, z, CORES + c)

                    @pl.when(x > 0)
                    def _():
                        pl.semaphore_wait(ready_d, CORES)

    acc[...] = jnp.zeros_like(acc)
    run_sum[...] = jnp.zeros_like(run_sum)
    run_max[...] = jnp.full_like(run_max, NEG)
    for c in (*list_copies, *q_copies):
        c.wait()

    def fill(r, carry):
        for p in range(slots):
            hit = jnp.int32(0)
            for s in range(slots):
                hit += jnp.where((lists[r, s] == p) & (s < counts[0, r]), 1, 0)
            bias[r * slots + p] = jnp.where(hit > 0, 0.0, NEG).astype(jnp.float32)
        return carry

    lax.fori_loop(0, n_row, fill, 0)

    def attend(j, count, masked, value_there):
        rows = count * block
        key = kbuf[pl.ds(j, count)].reshape(rows, head)
        s = lax.dot_general(
            key, q_stack[...], (((1,), (1,)), ((), ())), preferred_element_type=jnp.float32
        )
        if masked:
            key_row = lax.broadcasted_iota(jnp.int32, s.shape, 0)
            query_row = lax.broadcasted_iota(jnp.int32, s.shape, 1) % block
            s = jnp.where(key_row - query_row <= (mine - j) * block, s, NEG)
        old = run_max[...]
        parts = [s[b * block : (b + 1) * block] for b in range(count)]
        new = old
        for b in range(count):
            new = jnp.maximum(new, jnp.max(parts[b], axis=0, keepdims=True) + bias[j + b])
        w = jnp.concatenate(
            [jnp.exp2((parts[b] - (new - 3.0 * bias[j + b])) * factor) for b in range(count)], axis=0
        )
        decay = jnp.exp2((old - new) * factor)
        value_there()
        value = vbuf[pl.ds(j, count)].reshape(rows, head)
        run_max[...] = new
        run_sum[...] = run_sum[...] * decay + jnp.sum(w, axis=0, keepdims=True)
        acc[...] = acc[...] * decay + lax.dot_general(
            value, w.astype(jnp.bfloat16), (((0,), (0,)), ((), ())),
            preferred_element_type=jnp.float32,
        )

    def ahead_copies(r, part, act):
        j = r * n_col + col

        @pl.when((r == 0) & (z == 1) & (z + 1 < n_row) & (x > 0) & chip_wanted(j, z + 1, 0))
        def _():
            to = jnp.where(wanted(j, z + 1, k), k, CORES - 1)
            act(copy(j, part, send_e.at[part], z + 1, to))

    def relay_line(r, up):
        j = r * n_col + col

        @pl.when(on_line(j, z, x, r))
        def _():
            for part in range(2):
                arrived(j, part)
                if up or not short:
                    onward(r, up, (part,), start, (1,) if short else None)
                fan_out(r, (part,), start)

            if cross_first and up:
                for part in range(2):
                    ahead_copies(r, part, start)

    def passed_down(j):
        return (z == 2) & chip_wanted(j, 0, x) & jnp.logical_not(chip_wanted(j, 0, 1 - x))

    def own_receiver(j, kc):
        if kc == 0:
            return jnp.where(wanted(j, z, x * CORES), 0, 1) == k
        return k == 1

    def cross_own(act_wait, act_send, act_sibling):
        for kc in range(CORES):
            j = z * n_col + (1 - x) * CORES + kc

            @pl.when((x > 0) & passed_down(j) & own_receiver(j, kc))
            def _():
                for part in range(2):
                    act_wait(j, part)
                    act_send(copy(j, part, send_d.at[kc, part], 0, col))

                    if act_sibling is not None:
                        @pl.when((k == kc) & wanted(j, z, sibling))
                        def _():
                            act_sibling(s_copy(z, 1 - x, part))

    def relay_own():
        if cross_first:
            cross_own(arrived, start, start)
        relay_chips(z, 1)

    def relay_chips(r, up):
        for dx in range(1, n_x):
            cx = (x + dx) % n_x
            j = r * n_col + cx * CORES + k

            later = jnp.logical_not((r == z) & (x > 0) & passed_down(j)) if cross_first else True

            @pl.when(wanted(j, z, col) & wanted(j, z, sibling) & later)
            def _():
                for part in range(2):
                    arrived(j, part)
                    s_copy(r, cx, part).start()

    def attend_chips(r, dxs):
        for dx in dxs:
            first = r * n_col + ((x + dx) % n_x) * CORES
            theirs = first + 1 - k
            ours = first + k
            alone = wanted(ours, z, col) & jnp.logical_not(wanted(ours, z, sibling))
            sent = wanted(theirs, z, col)
            if cross_first and dx:
                early = (r == z) & (x > 0)
                alone &= jnp.logical_not(early & passed_down(ours))
                sent &= jnp.logical_not(early & passed_down(theirs) & jnp.logical_not(wanted(theirs, z, sibling)))

            def there(part):
                if dx:
                    @pl.when(alone)
                    def _():
                        arrived(ours, part)

                @pl.when(sent)
                def _():
                    arrived(theirs, part)

            there(0)

            @pl.when(first + CORES <= mine)
            def _():
                attend(first, CORES, False, lambda: there(1))

            for c in range(CORES):
                @pl.when(first + c == mine)
                def _():
                    attend(first, c + 1, True, lambda: there(1))

    def at_distance(d, act):
        for r, up in ((z - d, 1), (z + d, 0)):
            @pl.when((r >= 0) & (r < n_row) & ((up > 0) | (d > 0)))
            def _():
                act(r, up)

    def near(t, act, swap=True):
        d = t + jnp.where(t % REACH == 2, 1, 0) - jnp.where((t % REACH == 0) & (t > 0), 1, 0)
        at_distance(jnp.where(swap, d, t), act)

    def attend_near(r, up):
        attend_chips(r, (0,))

    def attend_far(r, up):
        attend_chips(r, range(1, n_x))

    attend_near(z, 1)
    at_distance(1, relay_line)
    relay_own()
    near(jnp.int32(2), relay_line)

    def settle_lines():
        if cross_first:
            for part in range(2):
                ahead_copies(0, part, wait_send)

        both_ways(z, (0, 1), wait_send)
        fan_out(z, (0, 1), wait_send)

        def drain(r, carry):
            @pl.when((r != z) & on_line(r * n_col + col, z, x, r))
            def _():
                if short:
                    @pl.when(r < z)
                    def _():
                        onward(r, 1, (0, 1), wait_send, (1,))
                else:
                    both_ways(r, (0, 1), wait_send)
                fan_out(r, (0, 1), wait_send)

            return carry

        lax.fori_loop(0, n_row, drain, 0)

    def settle_chips():
        if cross_first:
            cross_own(lambda j, part: None, wait_send, None)

        def drain(r, carry):
            for dx in range(1, n_x):
                cx = (x + dx) % n_x
                j = r * n_col + cx * CORES + k

                @pl.when(wanted(j, z, sibling) & wanted(j, z, col))
                def _():
                    for part in range(2):
                        s_copy(r, cx, part).wait_send()

            return carry

        lax.fori_loop(0, n_row, drain, 0)

    last = (n_row - 1 + REACH - 1) // REACH * REACH

    paired = (x > 0) | (z < REACH)
    late = (x > 0) & (z == 2) & (k == 0)

    def step(t, carry):
        near(jnp.where(late, n_row + REACH, t + 1), attend_near)
        near(t + 3, relay_line)
        pl.when(t == last - 2)(settle_lines)
        near(t + 1, relay_chips)
        near(jnp.where(late, t + 1, n_row + REACH), attend_near)
        near(t, attend_far, paired)
        return carry

    lax.fori_loop(0, last + 1, step, 0)
    settle_chips()

    inverse = 1.0 / run_sum[...]
    for h in range(heads):
        part = slice(h * block, (h + 1) * block)
        o_ref[0, :, h * head : (h + 1) * head] = (acc[:, part] * inverse[:, part]).astype(o_ref.dtype).T


def per_device(n_row, n_col, queries, keys, values, block_list, block_count):
    block, head = keys.shape[1], keys.shape[2]
    wide = queries.shape[1] * (queries.shape[2] // head)
    slots = block_list.shape[3]
    assert queries.shape[1] == block and slots == n_col and block_list.shape[1] == n_row
    blocks = n_row * n_col
    vmem = pl.BlockSpec(memory_space=pltpu.VMEM)
    hbm = pl.BlockSpec(memory_space=pl.ANY)
    return pl.pallas_call(
        functools.partial(kernel, n_row, n_col),
        out_shape=pltpu.VMEM(queries.shape, queries.dtype),
        in_specs=[hbm] * 5,
        out_specs=vmem,
        scratch_shapes=[
            pltpu.VMEM((blocks, block, head), keys.dtype),
            pltpu.VMEM((blocks, block, head), values.dtype),
            pltpu.VMEM((wide, head), queries.dtype),
            pltpu.VMEM((head, wide), jnp.float32),
            pltpu.VMEM((1, wide), jnp.float32),
            pltpu.VMEM((1, wide), jnp.float32),
            pltpu.SMEM((n_row, slots), jnp.int32),
            pltpu.SMEM((1, n_row), jnp.int32),
            pltpu.SMEM((blocks,), jnp.float32),
            pltpu.SemaphoreType.DMA((4 + wide // block,)),
            pltpu.SemaphoreType.DMA((blocks, 2)),
            pltpu.SemaphoreType.REGULAR((len(UP),)),
            pltpu.SemaphoreType.REGULAR((max(1, n_col // CORES - 1),)),
            pltpu.SemaphoreType.REGULAR,
            pltpu.SemaphoreType.DMA((n_row, 2, REACH, 2)),
            pltpu.SemaphoreType.DMA((n_row, n_col // CORES, 2)),
            pltpu.SemaphoreType.DMA((n_row, n_col // CORES, 2)),
            pltpu.SemaphoreType.DMA((CORES, 2)),
            pltpu.SemaphoreType.DMA((2,)),
        ],
        compiler_params=pltpu.CompilerParams(collective_id=0, has_side_effects=True),
        name="gather_attend",
    )(*(pltpu.with_memory_space_constraint(a, pltpu.HBM) for a in (queries, keys, values, block_list, block_count)))


def solution(mesh):
    placed = (
        P(("groups", "col"), "row", None),
        P(("groups", "row"), "col", None),
        P(("groups", "row"), "col", None),
        P("groups", None, None, None),
        P("groups", None, None),
    )
    return jax.shard_map(
        functools.partial(per_device, mesh.shape["row"], mesh.shape["col"]),
        mesh=mesh,
        in_specs=placed,
        out_specs=P(("groups", "col"), "row", None),
        check_vma=False,
    )
```
